256 devices in a mesh: facet: 4 (over z_lo, core), vis: 64 (over z_hi, y, x).
Axes of the slice: x: 4, y: 4, z: 8 (z_hi: 4, z_lo: 2; z = z_hi * 2 + z_lo), core: 2. Of those that a mesh axis runs over, the one named last changes fastest.
Arguments:
- visibilities: bfloat16 [2048, 128], P('vis'), may hold values from -6 to 6
- uv_coords: float32 [2048, 2], P('vis'), may hold values from -1280 to 1280
- cells: int32 [2, 2048, 64], P(None, 'vis'), may hold values from 0 to 4095
- centres: float32 [4, 2], P('facet'), may hold values from -0.03 to 0.03
- intersection_mask: int32 [4, 64, 256], P('facet', 'vis'), may hold values 0 or 1
Outputs:
- stitched: float32 [3, 64, 16384], P(None, 'vis', 'facet')
The draws below stay inside these ranges and needn't reach their ends.
All inputs are finite; a program needn't handle non-finite values. No bound on the sum of `intersection_mask` on one device may be relied on, other than what follows from the above.
Results may differ from the reference program's by a relative error of at most 0.0055.
Values may be sent and summed in bfloat16 or wider, within the bound.
No kernel may reach another device: no remote copies, remote signals or barrier semaphores. Data moves between devices by JAX's collectives and lax.ppermute only.
A program may use at most 64 MiB of HBM per device.

```python
import math
import jax
import jax.numpy as jnp
from jax import lax

GRID = 4096
CH = 64
TERMS = 3
OVER = 256
FACETS = 4
VIS_ROWS = 2048
IMG_ROWS = 64
VIS_ALL = 131072


def touch_ends(values, key, low, high):
    index_at = [jax.random.randint(jax.random.fold_in(key, axis), (), 0, length) for axis, length in enumerate(values.shape)]
    longest = values.shape.index(max(values.shape))
    beside = index_at[:longest] + [(index_at[longest] + 1) % values.shape[longest]] + index_at[longest + 1:]
    return values.at[tuple(index_at)].set(low).at[tuple(beside)].set(high)


def block_scale(stream_key, shape, pieces, least, high):
    factor_of = 1.0
    for axis_at, parts in pieces:
        heights = jax.random.uniform(jax.random.fold_in(jax.random.fold_in(stream_key, 6), axis_at), (parts,), jnp.float32, least / len(pieces), high / len(pieces))
        factor_of = factor_of * jnp.repeat(jnp.exp(heights), shape[axis_at] // parts).reshape((-1,) + (1,) * (len(shape) - 1 - axis_at))
    return factor_of


def scatter_about(rng, shape, spread, most, split=(), held_as=jnp.bfloat16):
    entries = jax.random.normal(rng, shape, jnp.float32) * spread
    if len(split) > 0:
        entries = block_scale(rng, shape, split, -0.22, 0.18) * entries
    return jnp.clip(entries, min=-most, max=most).astype(held_as)


def setup_inputs(seed: int = 0) -> dict:
    arg_keys = jax.random.split(jax.random.key(seed), 6)
    return {
        "visibilities": scatter_about(arg_keys[0], (VIS_ROWS, 2 * CH), 1.0, 6.0, ((0, 64),)),
        "uv_coords": scatter_about(arg_keys[1], (VIS_ROWS, 2), 200.0, 1280.0, ((0, 64),), jnp.float32),
        "cells": touch_ends(jax.random.randint(arg_keys[2], (2, VIS_ROWS, CH), 0, GRID), jax.random.fold_in(arg_keys[2], 1), 0, GRID - 1).astype(jnp.int32),
        "centres": jnp.clip(jax.random.uniform(arg_keys[3], (FACETS, 2), jnp.float32, -0.03, 0.03) * block_scale(arg_keys[3], (FACETS, 2), ((0, 4),), -0.4, 0.0), -0.03, 0.03),
        "intersection_mask": touch_ends((jax.random.randint(arg_keys[4], (FACETS, IMG_ROWS, OVER), 0, 4) < 3).astype(jnp.int32), jax.random.fold_in(arg_keys[4], 1), 0, 1),
    }


def channel_nu(chans):
    return (2.0 * jnp.arange(chans, dtype=jnp.float32) + 1.0 - chans) / chans

def rotate_rows(visibilities, uv_coords, centre):
    chans = visibilities.shape[1] // 2
    freq = 1.0 + 0.15 * channel_nu(chans)
    proj = uv_coords[:, 0:1] * centre[0] + uv_coords[:, 1:2] * centre[1]
    phase = 2.0 * math.pi * proj * freq[None, :]
    cosine = jnp.cos(phase)
    sine = jnp.sin(phase)
    real_part = visibilities[:, :chans].astype(jnp.float32)
    imag_part = visibilities[:, chans:].astype(jnp.float32)
    joined = jnp.concatenate([real_part * cosine + imag_part * sine, imag_part * cosine - real_part * sine], axis=1)
    return joined.astype(jnp.bfloat16)

def row_terms(rotated, cell_rows, first, count, img_rows, grid):
    chans = rotated.shape[1] // 2
    nu_vals = channel_nu(chans)
    power_list = [jnp.ones_like(nu_vals)]
    for term in range(TERMS - 1):
        power_list.append(power_list[-1] * nu_vals)
    powers = jnp.tile(jnp.stack(power_list), (1, rotated.shape[0]))
    offset = first + jnp.arange(count, dtype=jnp.int32) - img_rows // 2
    turns = jnp.mod(offset[:, None] * cell_rows[None, :], grid)
    alpha = turns.astype(jnp.float32) * (2.0 * math.pi / grid)
    cosine = jnp.cos(alpha)
    sine = jnp.sin(alpha)
    real_part = rotated[:, :chans].astype(jnp.float32).reshape(-1)
    imag_part = rotated[:, chans:].astype(jnp.float32).reshape(-1)
    base_real = cosine * real_part[None, :] - sine * imag_part[None, :]
    base_imag = cosine * imag_part[None, :] + sine * real_part[None, :]
    stacked = jnp.stack([base_real[:, None, :] * powers[None], base_imag[:, None, :] * powers[None]], axis=1)
    return stacked.astype(jnp.bfloat16)

def dft_table(grid, first, width):
    cell_index = jnp.arange(grid, dtype=jnp.int32)
    pixels = first + jnp.arange(width, dtype=jnp.int32) - grid // 2
    turns = jnp.mod(cell_index[:, None] * pixels[None, :], grid)
    theta = turns.astype(jnp.float32) * (2.0 * math.pi / grid)
    return jnp.concatenate([jnp.cos(theta), -jnp.sin(theta)], axis=0).astype(jnp.bfloat16)

def reference(visibilities, uv_coords, cells, centres, intersection_mask):
    cell_rows = cells[0].reshape(-1)
    cell_cols = cells[1].reshape(-1)
    scale = 1.0 / math.sqrt(VIS_ALL)
    table = dft_table(GRID, 0, GRID)
    ramp = 1.0 - (jnp.arange(OVER, dtype=jnp.float32) + 0.5) / OVER
    images = []
    for facet in range(FACETS):
        rotated = rotate_rows(visibilities, uv_coords, centres[facet])

        def one_row(row):
            values = row_terms(rotated, cell_rows, row, 1, IMG_ROWS, GRID)[0].astype(jnp.float32)
            flat = values.reshape(2 * TERMS, -1).T
            summed = jax.ops.segment_sum(flat, cell_cols, num_segments=GRID)
            return summed.T.reshape(2, TERMS, GRID)
        rowsum = lax.map(one_row, jnp.arange(IMG_ROWS, dtype=jnp.int32))
        left_side = rowsum.astype(jnp.bfloat16).transpose(0, 2, 1, 3).reshape(IMG_ROWS * TERMS, 2 * GRID)
        image = jnp.dot(left_side, table, preferred_element_type=jnp.float32)
        image = image.reshape(IMG_ROWS, TERMS, GRID).transpose(1, 0, 2) * scale
        images.append(image)
    blended = [images[0]]
    for facet in range(1, FACETS):
        own = images[facet]
        weight = intersection_mask[facet].astype(jnp.float32) * ramp[None, :]
        head = own[:, :, :OVER] + weight[None] * (images[facet - 1][:, :, GRID - OVER:] - own[:, :, :OVER])
        blended.append(jnp.concatenate([head, own[:, :, OVER:]], axis=2))
    return jnp.concatenate(blended, axis=2)
```

```python
import math

import jax
import jax.numpy as jnp
import numpy as np
from jax import lax
from jax.experimental import pallas as pl
from jax.experimental.pallas import tpu as pltpu
from jax.sharding import PartitionSpec as P

GRID = 4096
CH = 64
TERMS = 3
OVER = 256
FACETS = 4
VIS_ROWS = 2048
IMG_ROWS = 64
VIS_ALL = VIS_ROWS * CH
SIDE = 4
BLOCKS = SIDE * SIDE
ROWS = VIS_ROWS // IMG_ROWS
HALF = ROWS // 2
SECT = 7
FINE = 8
COARSE = GRID // 2 // FINE
XB = GRID // FINE
VALS = FACETS * TERMS
CHUNK = 32

COS = (0.99999999, -19.73920447, 64.93911593, -85.45011343, 60.16742979, -25.96688461, 6.52770596)
SIN = (6.28318491, -41.3415883, 81.59991362, -76.6141403, 41.34136538, -12.46881862)


def tables():
    gh = np.arange(COARSE)[:, None]
    xb = np.arange(XB)[None, :]
    ang = 2 * np.pi * ((gh * xb) % XB) / XB
    cosine, sine = np.cos(ang), np.sin(ang)
    first = np.concatenate(
        [np.concatenate([cosine, sine], 1), np.concatenate([-sine, cosine], 1)], 0
    )
    gl = np.arange(FINE)[:, None]
    tw = 2 * np.pi * (gl * xb) / GRID
    scale = np.where(gl % 2 == 0, 1.0, -1.0) / math.sqrt(VIS_ALL)
    twiddle = np.concatenate([np.cos(tw) * scale, np.sin(tw) * scale], 0)
    xa = np.arange(FINE)[:, None]
    turn = 2 * np.pi * ((xa * np.arange(FINE)[None, :]) % FINE) / FINE
    real, imag = np.cos(turn), -np.sin(turn)
    imag[:, 0] = 1.0
    eye = np.eye(VALS)
    second = np.concatenate([np.kron(eye, real), np.kron(eye, imag)], 1)
    return (
        jnp.asarray(first, jnp.bfloat16),
        jnp.asarray(twiddle, jnp.float32),
        jnp.asarray(second, jnp.float32),
    )


def turns_cos_sin(turns):
    frac = turns - jnp.round(turns)
    sq = frac * frac
    cosine = jnp.full_like(sq, COS[-1])
    for coef in COS[-2::-1]:
        cosine = cosine * sq + coef
    sine = jnp.full_like(sq, SIN[-1])
    for coef in SIN[-2::-1]:
        sine = sine * sq + coef
    return cosine, sine * frac


def pack_kernel(vis_ref, uv_ref, cells_ref, centre_ref, out_ref):
    lane = lax.broadcasted_iota(jnp.int32, (HALF, 2 * CH), 1)
    left = lane < CH
    vis = vis_ref[...].astype(jnp.float32)
    top, low = vis[:HALF], vis[HALF:]
    out_ref[0:16] = jnp.where(left, top, pltpu.roll(low, CH, 1)).astype(jnp.bfloat16)
    out_ref[16:32] = jnp.where(left, pltpu.roll(top, CH, 1), low).astype(jnp.bfloat16)
    for which in range(2):
        cells = cells_ref[which]
        both = jnp.concatenate([cells[:HALF], cells[HALF:]], 1)
        at = 32 + 32 * which
        out_ref[at : at + 16] = (both >> 6).astype(jnp.float32).astype(jnp.bfloat16)
        out_ref[at + 16 : at + 32] = (both & 63).astype(jnp.float32).astype(jnp.bfloat16)

    def pieces(value):
        high = value.astype(jnp.bfloat16).astype(jnp.float32)
        rest = value - high
        mid = rest.astype(jnp.bfloat16).astype(jnp.float32)
        return [high, mid, rest - mid]

    uv = uv_ref[...]
    cen = jnp.broadcast_to(centre_ref[...], (HALF, 2))
    zero = jnp.zeros((HALF, CH - 12), jnp.float32)
    whole = jnp.concatenate(
        pieces(uv[:HALF]) + pieces(cen) + [zero] + pieces(uv[HALF:]) + pieces(cen) + [zero], 1
    )
    out_ref[96:112] = whole.astype(jnp.bfloat16)


def grid_kernel(
    place_ref, blocks_ref, first_ref, twiddle_ref, second_ref, o0, o1, o2, o3,
    terms_ref, cell_ref, left0, left1, right0, right1, total_ref, image_ref,
):
    own, zpos, row = place_ref[0], place_ref[1], place_ref[2]
    lane = lax.broadcasted_iota(jnp.int32, (HALF, 2 * CH), 1)
    chan = (lane % CH).astype(jnp.float32)
    nu = (2.0 * chan + 1.0 - CH) / CH
    freq = 1.0 + 0.15 * nu
    nu2 = nu * nu
    step = (row - IMG_ROWS // 2).astype(jnp.float32) * (1.0 / GRID)
    fine_iota = lax.broadcasted_iota(jnp.int32, (FINE, 2 * CH), 0)
    coarse_iota = lax.broadcasted_iota(jnp.int32, (COARSE, 2 * CH), 0)

    def joined(section):
        return section + pltpu.roll(section, 2 * CH - 2, 1) + pltpu.roll(section, 2 * CH - 4, 1)

    cens = []
    for q in range(SIDE):
        sect = joined(blocks_ref[q * SIDE, 96:112].astype(jnp.float32))
        cens.append((sect[0:1, 6:7], sect[0:1, 7:8]))

    def build(block, left_ref, right_ref):
        def section(at):
            return blocks_ref[block, 16 * at : 16 * at + 16].astype(jnp.float32)

        real, imag = section(0), section(1)
        gr = section(2) * 64.0 + section(3)
        gc = section(4) * 64.0 + section(5)
        place = joined(section(6))
        is_left = lane < CH
        u = jnp.where(is_left, place[:, 0:1], place[:, CH : CH + 1])
        v = jnp.where(is_left, place[:, 1:2], place[:, CH + 1 : CH + 2])
        mid = (gc == float(GRID // 2)).astype(jnp.float32)
        folded = jnp.where(gc > GRID // 2, GRID - gc, gc * (1.0 - mid))
        sign = jnp.where(gc > GRID // 2, -1.0, jnp.where(folded == 0.0, 0.0, 1.0))
        cell = folded.astype(jnp.int32)
        cell_ref[0] = cell & (FINE - 1)
        cell_ref[1] = cell >> (FINE.bit_length() - 1)
        keep = 1.0 - mid
        ca, sa = turns_cos_sin(gr * step)
        for q in range(SIDE):
            proj = u * cens[q][0] + v * cens[q][1]
            cp, sp = turns_cos_sin(proj * freq)
            rr = (real * cp + imag * sp).astype(jnp.bfloat16).astype(jnp.float32)
            ri = (imag * cp - real * sp).astype(jnp.bfloat16).astype(jnp.float32)
            br = ca * rr - sa * ri
            bi = ca * ri + sa * rr
            bi = bi * sign + br * mid
            br = br * keep
            for part, base in ((0, br), (1, bi)):
                at = part * VALS + q * TERMS
                terms_ref[at] = base
                terms_ref[at + 1] = base * nu
                terms_ref[at + 2] = base * nu2
        for i in range(HALF):
            fine = jnp.broadcast_to(cell_ref[0, i : i + 1, :], (FINE, 2 * CH)) == fine_iota
            vals = jnp.broadcast_to(terms_ref[:, i : i + 1, :], (2 * VALS, FINE, 2 * CH))
            vals = jnp.where(fine[None], vals, 0.0)
            cols = slice(i * 2 * CH, (i + 1) * 2 * CH)
            left_ref[:, cols] = vals.reshape(2 * VALS * FINE, 2 * CH).astype(jnp.bfloat16)
            coarse = jnp.broadcast_to(cell_ref[1, i : i + 1, :], (COARSE, 2 * CH)) == coarse_iota
            right_ref[:, cols] = jnp.where(coarse, 1.0, 0.0).astype(jnp.bfloat16)

    def add(left_ref, right_ref):
        total_ref[...] += lax.dot_general(
            left_ref[...], right_ref[...], (((1,), (1,)), ((), ())),
            preferred_element_type=jnp.float32,
        )

    total_ref[...] = jnp.zeros_like(total_ref)
    build(0, left0, right0)

    def two(i, carry):
        add(left0, right0)
        build(2 * i + 1, left1, right1)
        add(left1, right1)
        build(jnp.minimum(2 * i + 2, BLOCKS - 1), left0, right0)
        return carry

    lax.fori_loop(0, BLOCKS // 2, two, 0)

    span = VALS * FINE
    total = jnp.concatenate([total_ref[0:span], total_ref[span : 2 * span]], 1)
    mixed = jnp.dot(total.astype(jnp.bfloat16), first_ref[...], preferred_element_type=jnp.float32)
    ur = mixed[:, :XB].reshape(VALS, FINE, XB)
    ui = mixed[:, XB:].reshape(VALS, FINE, XB)
    wr, wi = twiddle_ref[0:FINE][None], twiddle_ref[FINE : 2 * FINE][None]
    vr = ur * wr - ui * wi
    vi = ur * wi + ui * wr
    middle = total[:, COARSE : COARSE + 1].reshape(VALS, FINE, 1)
    odd = lax.broadcasted_iota(jnp.int32, (1, 1, XB), 2) % 2 == 1
    flip = jnp.where(odd, -1.0, 1.0) * (1.0 / math.sqrt(VIS_ALL))
    at_zero = lax.broadcasted_iota(jnp.int32, (1, FINE, XB), 1) == 0
    vi = jnp.where(at_zero, middle * flip, vi)
    both = jnp.concatenate([vr.reshape(span, XB), vi.reshape(span, XB)], 0)
    image_ref[...] = jnp.dot(
        second_ref[...], both, preferred_element_type=jnp.float32, precision=lax.Precision.HIGHEST
    )
    size = TERMS * FINE
    for s, out in enumerate((o0, o1, o2, o3)):
        facet = lax.rem(own + s, FACETS)
        spot = lax.rem(facet - zpos + FACETS, FACETS)
        before = lax.rem(facet - zpos + 2 * FACETS - 1, FACETS)
        out[0:size] = image_ref[pl.ds(pl.multiple_of(spot * size, 8), size), :]
        prior = image_ref[pl.ds(pl.multiple_of(before * size, 8), size), :]
        for term in range(TERMS):
            at = term * FINE + FINE - 1
            out[size + term : size + term + 1, 0:OVER] = prior[at : at + 1, XB - OVER :]


def blend_kernel(place_ref, p0, p1, p2, p3, mask_ref, out_ref):
    size = TERMS * FINE
    image = (p0[0:size] + p1[0:size]) + (p2[0:size] + p3[0:size])
    tail = slice(size, size + TERMS)
    strip = (p0[tail, 0:OVER] + p1[tail, 0:OVER]) + (p2[tail, 0:OVER] + p3[tail, 0:OVER])
    has_left = (place_ref[0] > 0).astype(jnp.float32)
    pixel = lax.broadcasted_iota(jnp.int32, (1, OVER), 1).astype(jnp.float32)
    ramp = 1.0 - (pixel + 0.5) / OVER
    weight = mask_ref[0].astype(jnp.float32) * ramp * has_left
    for term in range(TERMS):
        for xa in range(FINE):
            line = image[term * FINE + xa : term * FINE + xa + 1]
            if xa == 0:
                head = line[:, :OVER]
                head = head + weight * (strip[term : term + 1] - head)
                out_ref[term, :, 0:OVER] = head
                out_ref[term, :, OVER:XB] = line[:, OVER:]
            else:
                out_ref[term, :, xa * XB : (xa + 1) * XB] = line


def swap_pairs():
    pairs = []
    for facet in range(FACETS):
        for z in range(SIDE):
            for y in range(SIDE):
                for x in range(SIDE):
                    source = facet * IMG_ROWS + z * BLOCKS + y * SIDE + x
                    target = z * IMG_ROWS + ((facet - y) % FACETS) * BLOCKS + y * SIDE + x
                    pairs.append((source, target))
    return pairs


def per_device(visibilities, uv_coords, cells, centres, intersection_mask):
    vmem = pl.BlockSpec(memory_space=pltpu.VMEM)
    smem = pl.BlockSpec(memory_space=pltpu.SMEM)
    facet, spot = lax.axis_index("facet"), lax.axis_index("vis")
    place = jnp.stack([facet, spot // BLOCKS, spot]).astype(jnp.int32)
    packed = pl.pallas_call(
        pack_kernel,
        out_shape=jax.ShapeDtypeStruct((16 * SECT, 2 * CH), jnp.bfloat16),
        in_specs=[vmem] * 4,
        out_specs=vmem,
        name="pack",
    )(visibilities, uv_coords, cells, centres)
    packed = lax.ppermute(packed, ("facet", "vis"), swap_pairs())
    planes = [[z * BLOCKS + i for i in range(BLOCKS)] for z in range(SIDE)]
    blocks = lax.all_to_all(
        jnp.broadcast_to(packed[None], (BLOCKS,) + packed.shape),
        "vis", 0, 0, axis_index_groups=planes,
    )
    first, twiddle, second = tables()
    chunk = jax.ShapeDtypeStruct((CHUNK, XB), jnp.float32)
    span = 2 * VALS * FINE
    wide = ROWS * CH
    parts = pl.pallas_call(
        grid_kernel,
        out_shape=[chunk] * FACETS,
        in_specs=[smem] + [vmem] * 4,
        out_specs=[vmem] * FACETS,
        scratch_shapes=[
            pltpu.VMEM((2 * VALS, HALF, 2 * CH), jnp.float32),
            pltpu.VMEM((2, HALF, 2 * CH), jnp.int32),
            pltpu.VMEM((span, wide), jnp.bfloat16),
            pltpu.VMEM((span, wide), jnp.bfloat16),
            pltpu.VMEM((COARSE, wide), jnp.bfloat16),
            pltpu.VMEM((COARSE, wide), jnp.bfloat16),
            pltpu.VMEM((span, COARSE), jnp.float32),
            pltpu.VMEM((VALS * FINE, XB), jnp.float32),
        ],
        compiler_params=pltpu.CompilerParams(vmem_limit_bytes=40 << 20),
        name="grid",
    )(place, blocks, first, twiddle, second)
    got = [parts[0]]
    for s in range(1, FACETS):
        got.append(lax.ppermute(parts[s], "facet", [(i, (i + s) % FACETS) for i in range(FACETS)]))
    return pl.pallas_call(
        blend_kernel,
        out_shape=jax.ShapeDtypeStruct((TERMS, 1, GRID), jnp.float32),
        in_specs=[smem] + [vmem] * 5,
        out_specs=vmem,
        name="blend",
    )(place, *got, intersection_mask)


def solution(mesh):
    placed = (
        P("vis", None),
        P("vis", None),
        P(None, "vis", None),
        P("facet", None),
        P("facet", "vis", None),
    )
    return jax.shard_map(
        per_device, mesh=mesh, in_specs=placed, out_specs=P(None, "vis", "facet"), check_vma=False
    )
```

```python
import math

import jax
import jax.numpy as jnp
import numpy as np
from jax import lax
from jax.experimental import pallas as pl
from jax.experimental.pallas import tpu as pltpu
from jax.sharding import PartitionSpec as P

GRID = 4096
CH = 64
TERMS = 3
OVER = 256
FACETS = 4
VIS_ROWS = 2048
IMG_ROWS = 64
VIS_ALL = VIS_ROWS * CH
SIDE = 4
BLOCKS = SIDE * SIDE
ROWS = VIS_ROWS // IMG_ROWS
HALF = ROWS // 2
SECT = 7
FINE = 8
COARSE = GRID // 2 // FINE
XB = GRID // FINE
VALS = FACETS * TERMS
STEP = 256
CHUNK = 32

COS = (0.99999999, -19.73920447, 64.93911593, -85.45011343, 60.16742979, -25.96688461, 6.52770596)
SIN = (6.28318491, -41.3415883, 81.59991362, -76.6141403, 41.34136538, -12.46881862)


def tables():
    gh = np.arange(COARSE)[:, None]
    xb = np.arange(XB)[None, :]
    ang = 2 * np.pi * ((gh * xb) % XB) / XB
    cosine, sine = np.cos(ang), np.sin(ang)
    first = np.concatenate(
        [np.concatenate([cosine, sine], 1), np.concatenate([-sine, cosine], 1)], 0
    )
    gl = np.arange(FINE)[:, None]
    tw = 2 * np.pi * (gl * xb) / GRID
    scale = np.where(gl % 2 == 0, 1.0, -1.0) / math.sqrt(VIS_ALL)
    twiddle = np.concatenate([np.cos(tw) * scale, np.sin(tw) * scale], 0)
    xa = np.arange(FINE)[:, None]
    turn = 2 * np.pi * ((xa * np.arange(FINE)[None, :]) % FINE) / FINE
    real, imag = np.cos(turn), -np.sin(turn)
    imag[:, 0] = 1.0
    eye = np.eye(VALS)
    second = np.concatenate([np.kron(eye, real), np.kron(eye, imag)], 1)
    return (
        jnp.asarray(first, jnp.bfloat16),
        jnp.asarray(twiddle, jnp.float32),
        jnp.asarray(second, jnp.float32),
    )


def turns_cos_sin(turns):
    frac = turns - jnp.round(turns)
    sq = frac * frac
    cosine = jnp.full_like(sq, COS[-1])
    for coef in COS[-2::-1]:
        cosine = cosine * sq + coef
    sine = jnp.full_like(sq, SIN[-1])
    for coef in SIN[-2::-1]:
        sine = sine * sq + coef
    return cosine, sine * frac


def pack_kernel(vis_ref, uv_ref, cells_ref, centre_ref, out_ref):
    lane = lax.broadcasted_iota(jnp.int32, (HALF, 2 * CH), 1)
    left = lane < CH
    vis = vis_ref[...].astype(jnp.float32)
    top, low = vis[:HALF], vis[HALF:]
    out_ref[0:16] = jnp.where(left, top, pltpu.roll(low, CH, 1)).astype(jnp.bfloat16)
    out_ref[16:32] = jnp.where(left, pltpu.roll(top, CH, 1), low).astype(jnp.bfloat16)
    for which in range(2):
        cells = cells_ref[which]
        both = jnp.concatenate([cells[:HALF], cells[HALF:]], 1)
        at = 32 + 32 * which
        out_ref[at : at + 16] = (both >> 6).astype(jnp.float32).astype(jnp.bfloat16)
        out_ref[at + 16 : at + 32] = (both & 63).astype(jnp.float32).astype(jnp.bfloat16)

    def pieces(value):
        high = value.astype(jnp.bfloat16).astype(jnp.float32)
        rest = value - high
        mid = rest.astype(jnp.bfloat16).astype(jnp.float32)
        return high, mid, rest - mid

    split = jnp.concatenate(pieces(uv_ref[...]), 0).astype(jnp.bfloat16)
    spots = lax.broadcasted_iota(jnp.int32, (6, 2 * CH), 0)
    spots = spots == lax.broadcasted_iota(jnp.int32, (6, 2 * CH), 1)
    columns = lax.dot_general(
        split, spots.astype(jnp.float32).astype(jnp.bfloat16), (((0,), (0,)), ((), ())),
        preferred_element_type=jnp.float32,
    )
    cen = jnp.where(lane % 2 == 0, centre_ref[0:1, 0:1], centre_ref[0:1, 1:2])
    whole = columns[:HALF] + pltpu.roll(columns[HALF:], CH, 1)
    for i, piece in enumerate(pieces(cen)):
        whole = jnp.where(lane // 2 == 3 + i, piece, whole)
    out_ref[96:112] = whole.astype(jnp.bfloat16)


def grid_kernel(
    place_ref, blocks_ref, first_ref, twiddle_ref, second_ref, o0, o1, o2, o3,
    terms0, terms1, cells0, cells1, left0, left1, right0, right1, total_ref, image_ref,
    iota_ref,
):
    own, zpos, row = place_ref[0], place_ref[1], place_ref[2]
    lane = lax.broadcasted_iota(jnp.int32, (HALF, 2 * CH), 1)
    chan = (lane % CH).astype(jnp.float32)
    nu = (2.0 * chan + 1.0 - CH) / CH
    freq = 1.0 + 0.15 * nu
    nu2 = nu * nu
    step = (row - IMG_ROWS // 2).astype(jnp.float32) * (1.0 / GRID)
    count = lax.broadcasted_iota(jnp.int32, (COARSE, 2 * CH), 0)
    iota_ref[...] = count.astype(jnp.float32).astype(jnp.bfloat16)
    fine_iota = (count[: 2 * FINE] & (FINE - 1)).astype(jnp.float32).astype(jnp.bfloat16)
    one = jnp.ones((2 * FINE, 2 * CH), jnp.bfloat16)
    zero = jnp.zeros((2 * FINE, 2 * CH), jnp.bfloat16)

    def joined(section):
        return section + pltpu.roll(section, 2 * CH - 2, 1) + pltpu.roll(section, 2 * CH - 4, 1)

    cens = []
    for q in range(SIDE):
        sect = joined(blocks_ref[q * SIDE, 96:112].astype(jnp.float32))
        cens.append((sect[0:1, 6:7], sect[0:1, 7:8]))

    def elements(block, terms_ref, cell_ref):
        def section(at):
            return blocks_ref[block, 16 * at : 16 * at + 16].astype(jnp.float32)

        real, imag = section(0), section(1)
        gr = section(2) * 64.0 + section(3)
        gc = section(4) * 64.0 + section(5)
        place = joined(section(6))
        is_left = lane < CH
        u = jnp.where(is_left, place[:, 0:1], place[:, CH : CH + 1])
        v = jnp.where(is_left, place[:, 1:2], place[:, CH + 1 : CH + 2])
        mid = (gc == float(GRID // 2)).astype(jnp.float32)
        folded = jnp.where(gc > GRID // 2, GRID - gc, gc * (1.0 - mid))
        sign = jnp.where(gc > GRID // 2, -1.0, jnp.where(folded == 0.0, 0.0, 1.0))
        cell = folded.astype(jnp.int32)
        cell_ref[0] = (cell & (FINE - 1)).astype(jnp.float32)
        cell_ref[1] = (cell >> (FINE.bit_length() - 1)).astype(jnp.float32)
        keep = 1.0 - mid
        ca, sa = turns_cos_sin(gr * step)
        for q in range(SIDE):
            proj = u * cens[q][0] + v * cens[q][1]
            cp, sp = turns_cos_sin(proj * freq)
            rr = (real * cp + imag * sp).astype(jnp.bfloat16).astype(jnp.float32)
            ri = (imag * cp - real * sp).astype(jnp.bfloat16).astype(jnp.float32)
            br = ca * rr - sa * ri
            bi = ca * ri + sa * rr
            bi = bi * sign + br * mid
            br = br * keep
            for part, base in ((0, br), (1, bi)):
                at = part * VALS + q * TERMS
                terms_ref[at] = base
                terms_ref[at + 1] = base * nu
                terms_ref[at + 2] = base * nu2

    def expand(i, terms_ref, cell_ref, left_ref, right_ref):
        cols = slice(i * 2 * CH, (i + 1) * 2 * CH)
        fine = jnp.broadcast_to(cell_ref[0, i : i + 1, :], (2 * FINE, 2 * CH)).astype(jnp.bfloat16)
        here = fine == fine_iota
        vals = jnp.broadcast_to(terms_ref[:, i : i + 1, :], (2 * VALS, FINE, 2 * CH))
        vals = vals.reshape(2 * VALS * FINE, 2 * CH).astype(jnp.bfloat16)
        coarse = jnp.broadcast_to(cell_ref[1, i : i + 1, :], (2 * FINE, 2 * CH))
        coarse = coarse.astype(jnp.bfloat16)
        for m in range(VALS):
            rows = slice(m * 2 * FINE, (m + 1) * 2 * FINE)
            left_ref[rows, cols] = jnp.where(here, vals[rows], zero)
        for m in range(COARSE // (2 * FINE)):
            rows = slice(m * 2 * FINE, (m + 1) * 2 * FINE)
            right_ref[rows, cols] = jnp.where(coarse == iota_ref[rows], one, zero)

    def product(i, left_ref, right_ref):
        cols = slice(i * STEP, (i + 1) * STEP)
        return lax.dot_general(
            right_ref[:, cols], left_ref[:, cols], (((1,), (1,)), ((), ())),
            preferred_element_type=jnp.float32,
        )

    def turn(block, here, ahead):
        part = total_ref[...]
        per = STEP // (2 * CH)
        elements(block, here[0], here[1])
        for i in range(ROWS * CH // STEP):
            part = part + product(i, here[2], here[3])
            for j in range(per):
                expand(i * per + j, *ahead)
        total_ref[...] = part

    even, odd = (terms0, cells0, left0, right0), (terms1, cells1, left1, right1)
    total_ref[...] = jnp.zeros_like(total_ref)
    elements(0, terms0, cells0)
    for i in range(HALF):
        expand(i, *even)
    elements(1, terms1, cells1)

    def two(i, carry):
        turn(jnp.minimum(2 * i + 2, BLOCKS - 1), even, odd)
        turn(jnp.minimum(2 * i + 3, BLOCKS - 1), odd, even)
        return carry

    lax.fori_loop(0, BLOCKS // 2, two, 0)

    span = VALS * FINE
    flat = total_ref[...].T
    total = jnp.concatenate([flat[0:span], flat[span : 2 * span]], 1)
    mixed = jnp.dot(total.astype(jnp.bfloat16), first_ref[...], preferred_element_type=jnp.float32)
    ur = mixed[:, :XB].reshape(VALS, FINE, XB)
    ui = mixed[:, XB:].reshape(VALS, FINE, XB)
    wr, wi = twiddle_ref[0:FINE][None], twiddle_ref[FINE : 2 * FINE][None]
    vr = ur * wr - ui * wi
    vi = ur * wi + ui * wr
    middle = total[:, COARSE : COARSE + 1].reshape(VALS, FINE, 1)
    is_odd = lax.broadcasted_iota(jnp.int32, (1, 1, XB), 2) % 2 == 1
    flip = jnp.where(is_odd, -1.0, 1.0) * (1.0 / math.sqrt(VIS_ALL))
    at_zero = lax.broadcasted_iota(jnp.int32, (1, FINE, XB), 1) == 0
    vi = jnp.where(at_zero, middle * flip, vi)
    both = jnp.concatenate([vr.reshape(span, XB), vi.reshape(span, XB)], 0)
    image_ref[...] = jnp.dot(
        second_ref[...], both, preferred_element_type=jnp.float32, precision=lax.Precision.HIGHEST
    )
    size = TERMS * FINE
    for s, out in enumerate((o0, o1, o2, o3)):
        facet = lax.rem(own + s, FACETS)
        spot = lax.rem(facet - zpos + FACETS, FACETS)
        before = lax.rem(facet - zpos + 2 * FACETS - 1, FACETS)
        out[0:size] = image_ref[pl.ds(pl.multiple_of(spot * size, 8), size), :]
        prior = image_ref[pl.ds(pl.multiple_of(before * size, 8), size), :]
        for term in range(TERMS):
            at = term * FINE + FINE - 1
            out[size + term : size + term + 1, 0:OVER] = prior[at : at + 1, XB - OVER :]


def blend_kernel(place_ref, p0, p1, p2, p3, mask_ref, out_ref):
    size = TERMS * FINE
    image = (p0[0:size] + p1[0:size]) + (p2[0:size] + p3[0:size])
    tail = slice(size, size + TERMS)
    strip = (p0[tail, 0:OVER] + p1[tail, 0:OVER]) + (p2[tail, 0:OVER] + p3[tail, 0:OVER])
    has_left = (place_ref[0] > 0).astype(jnp.float32)
    pixel = lax.broadcasted_iota(jnp.int32, (1, OVER), 1).astype(jnp.float32)
    ramp = 1.0 - (pixel + 0.5) / OVER
    weight = mask_ref[0].astype(jnp.float32) * ramp * has_left
    for term in range(TERMS):
        for xa in range(FINE):
            line = image[term * FINE + xa : term * FINE + xa + 1]
            if xa == 0:
                head = line[:, :OVER]
                head = head + weight * (strip[term : term + 1] - head)
                out_ref[term, :, 0:OVER] = head
                out_ref[term, :, OVER:XB] = line[:, OVER:]
            else:
                out_ref[term, :, xa * XB : (xa + 1) * XB] = line


def swap_pairs():
    pairs = []
    for facet in range(FACETS):
        for z in range(SIDE):
            for y in range(SIDE):
                for x in range(SIDE):
                    source = facet * IMG_ROWS + z * BLOCKS + y * SIDE + x
                    target = z * IMG_ROWS + ((facet - y) % FACETS) * BLOCKS + y * SIDE + x
                    pairs.append((source, target))
    return pairs


def per_device(visibilities, uv_coords, cells, centres, intersection_mask):
    vmem = pl.BlockSpec(memory_space=pltpu.VMEM)
    smem = pl.BlockSpec(memory_space=pltpu.SMEM)
    facet, spot = lax.axis_index("facet"), lax.axis_index("vis")
    place = jnp.stack([facet, spot // BLOCKS, spot]).astype(jnp.int32)
    packed = pl.pallas_call(
        pack_kernel,
        out_shape=jax.ShapeDtypeStruct((16 * SECT, 2 * CH), jnp.bfloat16),
        in_specs=[vmem] * 4,
        out_specs=vmem,
        compiler_params=pltpu.CompilerParams(vmem_limit_bytes=2 << 20),
        name="pack",
    )(visibilities, uv_coords.T, cells, centres)
    packed = lax.ppermute(packed, ("facet", "vis"), swap_pairs())
    planes = [[z * BLOCKS + i for i in range(BLOCKS)] for z in range(SIDE)]
    blocks = lax.all_to_all(
        jnp.broadcast_to(packed[None], (BLOCKS,) + packed.shape),
        "vis", 0, 0, axis_index_groups=planes,
    )
    first, twiddle, second = tables()
    chunk = jax.ShapeDtypeStruct((CHUNK, XB), jnp.float32)
    span = 2 * VALS * FINE
    wide = ROWS * CH
    parts = pl.pallas_call(
        grid_kernel,
        out_shape=[chunk] * FACETS,
        in_specs=[smem] + [vmem] * 4,
        out_specs=[vmem] * FACETS,
        scratch_shapes=[
            pltpu.VMEM((2 * VALS, HALF, 2 * CH), jnp.float32),
            pltpu.VMEM((2 * VALS, HALF, 2 * CH), jnp.float32),
            pltpu.VMEM((2, HALF, 2 * CH), jnp.float32),
            pltpu.VMEM((2, HALF, 2 * CH), jnp.float32),
            pltpu.VMEM((span, wide), jnp.bfloat16),
            pltpu.VMEM((span, wide), jnp.bfloat16),
            pltpu.VMEM((COARSE, wide), jnp.bfloat16),
            pltpu.VMEM((COARSE, wide), jnp.bfloat16),
            pltpu.VMEM((COARSE, span), jnp.float32),
            pltpu.VMEM((VALS * FINE, XB), jnp.float32),
            pltpu.VMEM((COARSE, 2 * CH), jnp.bfloat16),
        ],
        compiler_params=pltpu.CompilerParams(vmem_limit_bytes=40 << 20),
        name="grid",
    )(place, blocks, first, twiddle, second)
    got = [parts[0]]
    for s in range(1, FACETS):
        got.append(lax.ppermute(parts[s], "facet", [(i, (i + s) % FACETS) for i in range(FACETS)]))
    return pl.pallas_call(
        blend_kernel,
        out_shape=jax.ShapeDtypeStruct((TERMS, 1, GRID), jnp.float32),
        in_specs=[smem] + [vmem] * 5,
        out_specs=vmem,
        compiler_params=pltpu.CompilerParams(vmem_limit_bytes=2 << 20),
        name="blend",
    )(place, *got, intersection_mask)


def solution(mesh):
    placed = (
        P("vis", None),
        P("vis", None),
        P(None, "vis", None),
        P("facet", None),
        P("facet", "vis", None),
    )
    return jax.shard_map(
        per_device, mesh=mesh, in_specs=placed, out_specs=P(None, "vis", "facet"), check_vma=False
    )
```

```python
import math

import jax
import jax.numpy as jnp
import numpy as np
from jax import lax
from jax.experimental import pallas as pl
from jax.experimental.pallas import tpu as pltpu
from jax.sharding import PartitionSpec as P

GRID = 4096
CH = 64
TERMS = 3
OVER = 256
FACETS = 4
VIS_ROWS = 2048
IMG_ROWS = 64
VIS_ALL = VIS_ROWS * CH
SIDE = 4
BLOCKS = SIDE * SIDE
ROWS = VIS_ROWS // IMG_ROWS
HALF = ROWS // 2
PACKED = 4 * HALF + 8
BEHIND = (0, -1, 1, 2)
FINE = 8
COARSE = GRID // 2 // FINE
XB = GRID // FINE
VALS = FACETS * TERMS
STEP = 256
CHUNK = 32

COS = (0.99999999, -19.73920447, 64.93911593, -85.45011343, 60.16742979, -25.96688461, 6.52770596)
SIN = (6.28318491, -41.3415883, 81.59991362, -76.6141403, 41.34136538, -12.46881862)


def tables():
    gh = np.arange(COARSE)[:, None]
    xb = np.arange(XB)[None, :]
    ang = 2 * np.pi * ((gh * xb) % XB) / XB
    cosine, sine = np.cos(ang), np.sin(ang)
    first = np.concatenate(
        [np.concatenate([cosine, sine], 1), np.concatenate([-sine, cosine], 1)], 0
    )
    gl = np.arange(FINE)[:, None]
    tw = 2 * np.pi * (gl * xb) / GRID
    scale = np.where(gl % 2 == 0, 1.0, -1.0) / math.sqrt(VIS_ALL)
    twiddle = np.concatenate([np.cos(tw) * scale, np.sin(tw) * scale], 0)
    xa = np.arange(FINE)[:, None]
    turn = 2 * np.pi * ((xa * np.arange(FINE)[None, :]) % FINE) / FINE
    real, imag = np.cos(turn), -np.sin(turn)
    imag[:, 0] = 1.0
    eye = np.eye(VALS)
    second = np.concatenate([np.kron(eye, real), np.kron(eye, imag)], 1)
    return (
        jnp.asarray(first, jnp.bfloat16),
        jnp.asarray(twiddle, jnp.float32),
        jnp.asarray(second, jnp.float32),
    )


def turns_cos_sin(turns):
    frac = turns - jnp.round(turns)
    sq = frac * frac
    cosine = jnp.full_like(sq, COS[-1])
    for coef in COS[-2::-1]:
        cosine = cosine * sq + coef
    sine = jnp.full_like(sq, SIN[-1])
    for coef in SIN[-2::-1]:
        sine = sine * sq + coef
    return cosine, sine * frac


def coded(cell):
    size = ((cell & 127) + 128) << ((cell >> 7) & 15)
    value = size.astype(jnp.float32)
    return jnp.where(cell >= GRID // 2, -value, value).astype(jnp.bfloat16)


def decoded(value):
    size = jnp.abs(value)
    high = jnp.where(value < 0.0, float(GRID // 2) - 128.0, -128.0)
    for step in (8, 4, 2, 1):
        over = size >= 128.0 * 2**step
        size = jnp.where(over, size * 2.0**-step, size)
        high = jnp.where(over, high + 128.0 * step, high)
    return size + high


def pack_kernel(
    vis_hbm, uv_hbm, cells_hbm, centre_hbm, out_ref, vis_ref, uv_ref, cells_ref, centre_ref, sems
):
    pairs = ((vis_hbm, vis_ref), (uv_hbm, uv_ref), (cells_hbm, cells_ref), (centre_hbm, centre_ref))
    copies = [pltpu.make_async_copy(a, b, sems.at[i]) for i, (a, b) in enumerate(pairs)]
    for copy in copies:
        copy.start()
    for copy in copies:
        copy.wait()
    lane = lax.broadcasted_iota(jnp.int32, (HALF, 2 * CH), 1)
    left = lane < CH
    vis = vis_ref[...].astype(jnp.float32)
    top, low = vis[:HALF], vis[HALF:]
    out_ref[0:16] = jnp.where(left, top, pltpu.roll(low, CH, 1)).astype(jnp.bfloat16)
    out_ref[16:32] = jnp.where(left, pltpu.roll(top, CH, 1), low).astype(jnp.bfloat16)
    for which in range(2):
        cells = cells_ref[which]
        both = jnp.concatenate([cells[:HALF], cells[HALF:]], 1)
        out_ref[32 + 16 * which : 48 + 16 * which] = coded(both)

    def pieces(value):
        high = value.astype(jnp.bfloat16).astype(jnp.float32)
        rest = value - high
        mid = rest.astype(jnp.bfloat16).astype(jnp.float32)
        return high, mid, rest - mid

    split = jnp.concatenate(pieces(uv_ref[...]), 0).astype(jnp.bfloat16)
    spots = lax.broadcasted_iota(jnp.int32, (6, 2 * CH), 0)
    spots = spots == lax.broadcasted_iota(jnp.int32, (6, 2 * CH), 1)
    columns = lax.dot_general(
        split, spots.astype(jnp.float32).astype(jnp.bfloat16), (((0,), (0,)), ((), ())),
        preferred_element_type=jnp.float32,
    )
    whole = columns[0:8]
    for i in (1, 2, 3):
        whole = whole + pltpu.roll(columns[8 * i : 8 * i + 8], 32 * i, 1)
    lane = lane[0:8]
    cen = jnp.where(lane % 2 == 0, centre_ref[0:1, 0:1], centre_ref[0:1, 1:2])
    for i, piece in enumerate(pieces(cen)):
        whole = jnp.where(lane // 2 == 3 + i, piece, whole)
    out_ref[64:72] = whole.astype(jnp.bfloat16)


def grid_kernel(
    place_ref, blocks_ref, own_ref, pair_ref, first_ref, twiddle_ref, second_ref, o0, o1, o2, o3,
    terms0, terms1, cells0, cells1, left0, left1, right0, right1, total_ref, image_ref,
    iota_ref,
):
    own, row = place_ref[0], place_ref[1]
    lane = lax.broadcasted_iota(jnp.int32, (HALF, 2 * CH), 1)
    chan = (lane % CH).astype(jnp.float32)
    nu = (2.0 * chan + 1.0 - CH) / CH
    freq = 1.0 + 0.15 * nu
    nu2 = nu * nu
    step = (row - IMG_ROWS // 2).astype(jnp.float32) * (1.0 / GRID)
    count = lax.broadcasted_iota(jnp.int32, (COARSE, 2 * CH), 0)
    iota_ref[...] = count.astype(jnp.float32).astype(jnp.bfloat16)
    fine_iota = (count[: 2 * FINE] & (FINE - 1)).astype(jnp.float32).astype(jnp.bfloat16)
    one = jnp.ones((2 * FINE, 2 * CH), jnp.bfloat16)
    zero = jnp.zeros((2 * FINE, 2 * CH), jnp.bfloat16)

    def joined(section):
        return section + pltpu.roll(section, 2 * CH - 2, 1) + pltpu.roll(section, 2 * CH - 4, 1)

    cens = []
    for y in range(2):
        sect = joined(blocks_ref[y * SIDE, 64:72].astype(jnp.float32))
        cens.append((sect[0:1, 6:7], sect[0:1, 7:8]))
    for ref in (own_ref, pair_ref):
        cens.append((ref[0:1, 0:1], ref[0:1, 1:2]))

    def elements(block, terms_ref, cell_ref):
        def section(at):
            return blocks_ref[block, 16 * at : 16 * at + 16].astype(jnp.float32)

        real, imag = section(0), section(1)
        gr, gc = decoded(section(2)), decoded(section(3))
        place = joined(blocks_ref[block, 64:72].astype(jnp.float32))
        is_left = lane[0:8] < CH

        def column(at):
            both = [
                jnp.where(is_left, place[:, i : i + 1], place[:, CH + i : CH + i + 1])
                for i in (at, at + 32)
            ]
            return jnp.concatenate(both, 0)

        u, v = column(0), column(1)
        mid = (gc == float(GRID // 2)).astype(jnp.float32)
        folded = jnp.where(gc > GRID // 2, GRID - gc, gc * (1.0 - mid))
        sign = jnp.where(gc > GRID // 2, -1.0, jnp.where(folded == 0.0, 0.0, 1.0))
        cell = folded.astype(jnp.int32)
        cell_ref[0] = (cell & (FINE - 1)).astype(jnp.float32)
        cell_ref[1] = (cell >> (FINE.bit_length() - 1)).astype(jnp.float32)
        keep = 1.0 - mid
        ca, sa = turns_cos_sin(gr * step)
        for q in range(SIDE):
            proj = u * cens[q][0] + v * cens[q][1]
            cp, sp = turns_cos_sin(proj * freq)
            rr = (real * cp + imag * sp).astype(jnp.bfloat16).astype(jnp.float32)
            ri = (imag * cp - real * sp).astype(jnp.bfloat16).astype(jnp.float32)
            br = ca * rr - sa * ri
            bi = ca * ri + sa * rr
            bi = bi * sign + br * mid
            br = br * keep
            for part, base in ((0, br), (1, bi)):
                at = part * VALS + q * TERMS
                terms_ref[at] = base
                terms_ref[at + 1] = base * nu
                terms_ref[at + 2] = base * nu2

    def expand(i, terms_ref, cell_ref, left_ref, right_ref):
        cols = slice(i * 2 * CH, (i + 1) * 2 * CH)
        fine = jnp.broadcast_to(cell_ref[0, i : i + 1, :], (2 * FINE, 2 * CH)).astype(jnp.bfloat16)
        here = fine == fine_iota
        vals = jnp.broadcast_to(terms_ref[:, i : i + 1, :], (2 * VALS, FINE, 2 * CH))
        vals = vals.reshape(2 * VALS * FINE, 2 * CH).astype(jnp.bfloat16)
        coarse = jnp.broadcast_to(cell_ref[1, i : i + 1, :], (2 * FINE, 2 * CH))
        coarse = coarse.astype(jnp.bfloat16)
        for m in range(VALS):
            rows = slice(m * 2 * FINE, (m + 1) * 2 * FINE)
            left_ref[rows, cols] = jnp.where(here, vals[rows], zero)
        for m in range(COARSE // (2 * FINE)):
            rows = slice(m * 2 * FINE, (m + 1) * 2 * FINE)
            right_ref[rows, cols] = jnp.where(coarse == iota_ref[rows], one, zero)

    def product(i, left_ref, right_ref):
        cols = slice(i * STEP, (i + 1) * STEP)
        return lax.dot_general(
            right_ref[:, cols], left_ref[:, cols], (((1,), (1,)), ((), ())),
            preferred_element_type=jnp.float32,
        )

    def turn(block, here, ahead):
        part = total_ref[...]
        per = STEP // (2 * CH)
        elements(block, here[0], here[1])
        for i in range(ROWS * CH // STEP):
            part = part + product(i, here[2], here[3])
            for j in range(per):
                expand(i * per + j, *ahead)
        total_ref[...] = part

    even, odd = (terms0, cells0, left0, right0), (terms1, cells1, left1, right1)
    total_ref[...] = jnp.zeros_like(total_ref)
    elements(0, terms0, cells0)
    for i in range(HALF):
        expand(i, *even)
    elements(1, terms1, cells1)

    def two(i, carry):
        turn(jnp.minimum(2 * i + 2, BLOCKS - 1), even, odd)
        turn(jnp.minimum(2 * i + 3, BLOCKS - 1), odd, even)
        return carry

    lax.fori_loop(0, BLOCKS // 2, two, 0)

    span = VALS * FINE
    flat = total_ref[...].T
    total = jnp.concatenate([flat[0:span], flat[span : 2 * span]], 1)
    mixed = jnp.dot(total.astype(jnp.bfloat16), first_ref[...], preferred_element_type=jnp.float32)
    ur = mixed[:, :XB].reshape(VALS, FINE, XB)
    ui = mixed[:, XB:].reshape(VALS, FINE, XB)
    wr, wi = twiddle_ref[0:FINE][None], twiddle_ref[FINE : 2 * FINE][None]
    vr = ur * wr - ui * wi
    vi = ur * wi + ui * wr
    middle = total[:, COARSE : COARSE + 1].reshape(VALS, FINE, 1)
    is_odd = lax.broadcasted_iota(jnp.int32, (1, 1, XB), 2) % 2 == 1
    flip = jnp.where(is_odd, -1.0, 1.0) * (1.0 / math.sqrt(VIS_ALL))
    at_zero = lax.broadcasted_iota(jnp.int32, (1, FINE, XB), 1) == 0
    vi = jnp.where(at_zero, middle * flip, vi)
    both = jnp.concatenate([vr.reshape(span, XB), vi.reshape(span, XB)], 0)
    image_ref[...] = jnp.dot(
        second_ref[...], both, preferred_element_type=jnp.float32, precision=lax.Precision.HIGHEST
    )
    size = TERMS * FINE
    for s, out in enumerate((o0, o1, o2, o3)):
        spot = (2, 3, 1, 0)[s]
        before = ((own ^ s) + FACETS - 1) % FACETS ^ own
        before = jnp.where(before < 2, before + 2, 3 - before)
        out[0:size] = image_ref[spot * size : (spot + 1) * size]
        prior = image_ref[pl.ds(pl.multiple_of(before * size, 8), size), :]
        for term in range(TERMS):
            at = term * FINE + FINE - 1
            out[size + term : size + term + 1, 0:OVER] = prior[at : at + 1, XB - OVER :]


def blend_kernel(place_ref, p0, p1, p2, p3, mask_ref, out_ref):
    size = TERMS * FINE
    image = (p0[0:size] + p1[0:size]) + (p2[0:size] + p3[0:size])
    tail = slice(size, size + TERMS)
    strip = (p0[tail, 0:OVER] + p1[tail, 0:OVER]) + (p2[tail, 0:OVER] + p3[tail, 0:OVER])
    has_left = (place_ref[0] > 0).astype(jnp.float32)
    pixel = lax.broadcasted_iota(jnp.int32, (1, OVER), 1).astype(jnp.float32)
    ramp = 1.0 - (pixel + 0.5) / OVER
    weight = mask_ref[0].astype(jnp.float32) * ramp * has_left
    for term in range(TERMS):
        for xa in range(FINE):
            line = image[term * FINE + xa : term * FINE + xa + 1]
            if xa == 0:
                head = line[:, :OVER]
                head = head + weight * (strip[term : term + 1] - head)
                out_ref[term, :, 0:OVER] = head
                out_ref[term, :, OVER:XB] = line[:, OVER:]
            else:
                out_ref[term, :, xa * XB : (xa + 1) * XB] = line


def swap_pairs():
    pairs = []
    for facet in range(FACETS):
        for z in range(SIDE):
            for y in range(SIDE):
                for x in range(SIDE):
                    here = y * SIDE + x
                    plane = (z + BEHIND[facet]) % SIDE
                    source = ((3 - facet) ^ (y & 1)) * IMG_ROWS + plane * BLOCKS + here
                    pairs.append((source, facet * IMG_ROWS + z * BLOCKS + here))
    return pairs


def per_device(visibilities, uv_coords, cells, centres, intersection_mask):
    vmem = pl.BlockSpec(memory_space=pltpu.VMEM)
    smem = pl.BlockSpec(memory_space=pltpu.SMEM)
    hbm = pl.BlockSpec(memory_space=pltpu.HBM)
    facet, spot = lax.axis_index("facet"), lax.axis_index("vis")
    place = jnp.stack([facet, spot]).astype(jnp.int32)
    given = (visibilities, uv_coords.T, cells, centres)
    packed = pl.pallas_call(
        pack_kernel,
        out_shape=jax.ShapeDtypeStruct((PACKED, 2 * CH), jnp.bfloat16),
        in_specs=[hbm] * 4,
        out_specs=vmem,
        scratch_shapes=[pltpu.VMEM(one.shape, one.dtype) for one in given]
        + [pltpu.SemaphoreType.DMA((4,))],
        compiler_params=pltpu.CompilerParams(vmem_limit_bytes=63 << 20),
        name="pack",
    )(*given)
    packed = lax.ppermute(packed, ("facet", "vis"), swap_pairs())
    packed, centre = lax.optimization_barrier((packed, centres))
    pair = lax.ppermute(centre, "facet", [(i, i ^ 1) for i in range(FACETS)])
    planes = [[z * BLOCKS + i for i in range(BLOCKS)] for z in range(SIDE)]
    blocks = lax.all_to_all(
        jnp.broadcast_to(packed[None], (BLOCKS,) + packed.shape),
        "vis", 0, 0, axis_index_groups=planes,
    )
    first, twiddle, second = tables()
    chunk = jax.ShapeDtypeStruct((CHUNK, XB), jnp.float32)
    span = 2 * VALS * FINE
    wide = ROWS * CH
    parts = pl.pallas_call(
        grid_kernel,
        out_shape=[chunk] * FACETS,
        in_specs=[smem] + [vmem] * 6,
        out_specs=[vmem] * FACETS,
        scratch_shapes=[
            pltpu.VMEM((2 * VALS, HALF, 2 * CH), jnp.float32),
            pltpu.VMEM((2 * VALS, HALF, 2 * CH), jnp.float32),
            pltpu.VMEM((2, HALF, 2 * CH), jnp.float32),
            pltpu.VMEM((2, HALF, 2 * CH), jnp.float32),
            pltpu.VMEM((span, wide), jnp.bfloat16),
            pltpu.VMEM((span, wide), jnp.bfloat16),
            pltpu.VMEM((COARSE, wide), jnp.bfloat16),
            pltpu.VMEM((COARSE, wide), jnp.bfloat16),
            pltpu.VMEM((COARSE, span), jnp.float32),
            pltpu.VMEM((VALS * FINE, XB), jnp.float32),
            pltpu.VMEM((COARSE, 2 * CH), jnp.bfloat16),
        ],
        compiler_params=pltpu.CompilerParams(vmem_limit_bytes=40 << 20),
        name="grid",
    )(place, blocks, centres, pair, first, twiddle, second)
    got = [parts[0]]
    for s in range(1, FACETS):
        got.append(lax.ppermute(parts[s], "facet", [(i, i ^ s) for i in range(FACETS)]))
    return pl.pallas_call(
        blend_kernel,
        out_shape=jax.ShapeDtypeStruct((TERMS, 1, GRID), jnp.float32),
        in_specs=[smem] + [vmem] * 5,
        out_specs=vmem,
        compiler_params=pltpu.CompilerParams(vmem_limit_bytes=2 << 20),
        name="blend",
    )(place, *got, intersection_mask)


def solution(mesh):
    placed = (
        P("vis", None),
        P("vis", None),
        P(None, "vis", None),
        P("facet", None),
        P("facet", "vis", None),
    )
    return jax.shard_map(
        per_device, mesh=mesh, in_specs=placed, out_specs=P(None, "vis", "facet"), check_vma=False
    )
```

```python
import math

import jax
import jax.numpy as jnp
import numpy as np
from jax import lax
from jax.experimental import pallas as pl
from jax.experimental.pallas import tpu as pltpu
from jax.sharding import PartitionSpec as P

GRID = 4096
CH = 64
TERMS = 3
OVER = 256
FACETS = 4
VIS_ROWS = 2048
IMG_ROWS = 64
VIS_ALL = VIS_ROWS * CH
SIDE = 4
BLOCKS = SIDE * SIDE
ROWS = VIS_ROWS // IMG_ROWS
HALF = ROWS // 2
PACKED = 4 * HALF + 8
BEHIND = (0, -1, 1, 2)
FINE = 8
COARSE = GRID // 2 // FINE
XB = GRID // FINE
VALS = FACETS * TERMS
STEP = 256
CHUNK = 32

COS = (0.99999999, -19.73920447, 64.93911593, -85.45011343, 60.16742979, -25.96688461, 6.52770596)
SIN = (6.28318491, -41.3415883, 81.59991362, -76.6141403, 41.34136538, -12.46881862)


def tables():
    gh = np.arange(COARSE)[:, None]
    xb = np.arange(XB)[None, :]
    ang = 2 * np.pi * ((gh * xb) % XB) / XB
    cosine, sine = np.cos(ang), np.sin(ang)
    first = np.concatenate(
        [np.concatenate([cosine, sine], 1), np.concatenate([-sine, cosine], 1)], 0
    )
    gl = np.arange(FINE)[:, None]
    tw = 2 * np.pi * (gl * xb) / GRID
    scale = np.where(gl % 2 == 0, 1.0, -1.0) / math.sqrt(VIS_ALL)
    twiddle = np.concatenate([np.cos(tw) * scale, np.sin(tw) * scale], 0)
    xa = np.arange(FINE)[:, None]
    turn = 2 * np.pi * ((xa * np.arange(FINE)[None, :]) % FINE) / FINE
    real, imag = np.cos(turn), -np.sin(turn)
    imag[:, 0] = 1.0
    eye = np.eye(VALS)
    second = np.concatenate([np.kron(eye, real), np.kron(eye, imag)], 1)
    return (
        jnp.asarray(first, jnp.bfloat16),
        jnp.asarray(twiddle, jnp.float32),
        jnp.asarray(second, jnp.float32),
    )


def turns_cos_sin(turns):
    frac = turns - jnp.round(turns)
    sq = frac * frac
    cosine = jnp.full_like(sq, COS[-1])
    for coef in COS[-2::-1]:
        cosine = cosine * sq + coef
    sine = jnp.full_like(sq, SIN[-1])
    for coef in SIN[-2::-1]:
        sine = sine * sq + coef
    return cosine, sine * frac


def coded(cell):
    size = ((cell & 127) + 128) << ((cell >> 7) & 15)
    value = size.astype(jnp.float32)
    return jnp.where(cell >= GRID // 2, -value, value).astype(jnp.bfloat16)


def decoded(value):
    size = jnp.abs(value)
    high = jnp.where(value < 0.0, float(GRID // 2) - 128.0, -128.0)
    for step in (8, 4, 2, 1):
        over = size >= 128.0 * 2**step
        size = jnp.where(over, size * 2.0**-step, size)
        high = jnp.where(over, high + 128.0 * step, high)
    return size + high


def pack_kernel(
    vis_hbm, uv_hbm, cells_hbm, centre_hbm, out_ref, vis_ref, uv_ref, cells_ref, centre_ref, sems
):
    pairs = ((vis_hbm, vis_ref), (uv_hbm, uv_ref), (cells_hbm, cells_ref), (centre_hbm, centre_ref))
    copies = [pltpu.make_async_copy(a, b, sems.at[i]) for i, (a, b) in enumerate(pairs)]
    for copy in copies:
        copy.start()
    for copy in copies:
        copy.wait()
    lane = lax.broadcasted_iota(jnp.int32, (HALF, 2 * CH), 1)
    left = lane < CH
    vis = vis_ref[...].astype(jnp.float32)
    top, low = vis[:HALF], vis[HALF:]
    out_ref[0:16] = jnp.where(left, top, pltpu.roll(low, CH, 1)).astype(jnp.bfloat16)
    out_ref[16:32] = jnp.where(left, pltpu.roll(top, CH, 1), low).astype(jnp.bfloat16)
    for which in range(2):
        cells = cells_ref[which]
        both = jnp.concatenate([cells[:HALF], cells[HALF:]], 1)
        out_ref[32 + 16 * which : 48 + 16 * which] = coded(both)

    def pieces(value):
        high = value.astype(jnp.bfloat16).astype(jnp.float32)
        rest = value - high
        mid = rest.astype(jnp.bfloat16).astype(jnp.float32)
        return high, mid, rest - mid

    split = jnp.concatenate(pieces(uv_ref[...]), 0).astype(jnp.bfloat16)
    spots = lax.broadcasted_iota(jnp.int32, (6, 2 * CH), 0)
    spots = spots == lax.broadcasted_iota(jnp.int32, (6, 2 * CH), 1)
    columns = lax.dot_general(
        split, spots.astype(jnp.float32).astype(jnp.bfloat16), (((0,), (0,)), ((), ())),
        preferred_element_type=jnp.float32,
    )
    whole = columns[0:8]
    for i in (1, 2, 3):
        whole = whole + pltpu.roll(columns[8 * i : 8 * i + 8], 32 * i, 1)
    lane = lane[0:8]
    cen = jnp.where(lane % 2 == 0, centre_ref[0:1, 0:1], centre_ref[0:1, 1:2])
    for i, piece in enumerate(pieces(cen)):
        whole = jnp.where(lane // 2 == 3 + i, piece, whole)
    out_ref[64:72] = whole.astype(jnp.bfloat16)


def spread_kernel(block_ref, out_ref):
    for i in range(BLOCKS):
        out_ref[i] = block_ref[...]


def grid_kernel(
    place_ref, blocks_ref, own_ref, pair_ref, first_hbm, twiddle_ref, second_ref, o0, o1, o2, o3,
    terms0, terms1, cells0, cells1, left0, left1, right0, right1, total_ref, image_ref,
    iota_ref, first_ref, sem,
):
    table = pltpu.make_async_copy(first_hbm, first_ref, sem)
    table.start()
    own, row = place_ref[0], place_ref[1]
    lane = lax.broadcasted_iota(jnp.int32, (HALF, 2 * CH), 1)
    chan = (lane % CH).astype(jnp.float32)
    nu = (2.0 * chan + 1.0 - CH) / CH
    freq = 1.0 + 0.15 * nu
    nu2 = nu * nu
    step = (row - IMG_ROWS // 2).astype(jnp.float32) * (1.0 / GRID)
    count = lax.broadcasted_iota(jnp.int32, (COARSE, 2 * CH), 0)
    iota_ref[...] = count.astype(jnp.float32).astype(jnp.bfloat16)
    fine_iota = (count[: 2 * FINE] & (FINE - 1)).astype(jnp.float32).astype(jnp.bfloat16)
    one = jnp.ones((2 * FINE, 2 * CH), jnp.bfloat16)
    zero = jnp.zeros((2 * FINE, 2 * CH), jnp.bfloat16)

    def joined(section):
        return section + pltpu.roll(section, 2 * CH - 2, 1) + pltpu.roll(section, 2 * CH - 4, 1)

    cens = []
    for y in range(2):
        sect = joined(blocks_ref[y * SIDE, 64:72].astype(jnp.float32))
        cens.append((sect[0:1, 6:7], sect[0:1, 7:8]))
    for ref in (own_ref, pair_ref):
        cens.append((ref[0:1, 0:1], ref[0:1, 1:2]))

    def elements(block, terms_ref, cell_ref):
        def section(at):
            return blocks_ref[block, 16 * at : 16 * at + 16].astype(jnp.float32)

        real, imag = section(0), section(1)
        gr, gc = decoded(section(2)), decoded(section(3))
        place = joined(blocks_ref[block, 64:72].astype(jnp.float32))
        is_left = lane[0:8] < CH

        def column(at):
            both = [
                jnp.where(is_left, place[:, i : i + 1], place[:, CH + i : CH + i + 1])
                for i in (at, at + 32)
            ]
            return jnp.concatenate(both, 0)

        u, v = column(0), column(1)
        mid = (gc == float(GRID // 2)).astype(jnp.float32)
        folded = jnp.where(gc > GRID // 2, GRID - gc, gc * (1.0 - mid))
        sign = jnp.where(gc > GRID // 2, -1.0, jnp.where(folded == 0.0, 0.0, 1.0))
        cell = folded.astype(jnp.int32)
        cell_ref[0] = (cell & (FINE - 1)).astype(jnp.float32)
        cell_ref[1] = (cell >> (FINE.bit_length() - 1)).astype(jnp.float32)
        keep = 1.0 - mid
        ca, sa = turns_cos_sin(gr * step)
        for q in range(SIDE):
            proj = u * cens[q][0] + v * cens[q][1]
            cp, sp = turns_cos_sin(proj * freq)
            rr = (real * cp + imag * sp).astype(jnp.bfloat16).astype(jnp.float32)
            ri = (imag * cp - real * sp).astype(jnp.bfloat16).astype(jnp.float32)
            br = ca * rr - sa * ri
            bi = ca * ri + sa * rr
            bi = bi * sign + br * mid
            br = br * keep
            for part, base in ((0, br), (1, bi)):
                at = part * VALS + q * TERMS
                terms_ref[at] = base
                terms_ref[at + 1] = base * nu
                terms_ref[at + 2] = base * nu2

    def expand(i, terms_ref, cell_ref, left_ref, right_ref):
        cols = slice(i * 2 * CH, (i + 1) * 2 * CH)
        fine = jnp.broadcast_to(cell_ref[0, i : i + 1, :], (2 * FINE, 2 * CH)).astype(jnp.bfloat16)
        here = fine == fine_iota
        vals = jnp.broadcast_to(terms_ref[:, i : i + 1, :], (2 * VALS, FINE, 2 * CH))
        vals = vals.reshape(2 * VALS * FINE, 2 * CH).astype(jnp.bfloat16)
        coarse = jnp.broadcast_to(cell_ref[1, i : i + 1, :], (2 * FINE, 2 * CH))
        coarse = coarse.astype(jnp.bfloat16)
        for m in range(VALS):
            rows = slice(m * 2 * FINE, (m + 1) * 2 * FINE)
            left_ref[rows, cols] = jnp.where(here, vals[rows], zero)
        for m in range(COARSE // (2 * FINE)):
            rows = slice(m * 2 * FINE, (m + 1) * 2 * FINE)
            right_ref[rows, cols] = jnp.where(coarse == iota_ref[rows], one, zero)

    def product(i, left_ref, right_ref):
        cols = slice(i * STEP, (i + 1) * STEP)
        return lax.dot_general(
            right_ref[:, cols], left_ref[:, cols], (((1,), (1,)), ((), ())),
            preferred_element_type=jnp.float32,
        )

    def turn(block, here, ahead):
        part = total_ref[...]
        per = STEP // (2 * CH)
        elements(block, here[0], here[1])
        for i in range(ROWS * CH // STEP):
            part = part + product(i, here[2], here[3])
            for j in range(per):
                expand(i * per + j, *ahead)
        total_ref[...] = part

    even, odd = (terms0, cells0, left0, right0), (terms1, cells1, left1, right1)
    total_ref[...] = jnp.zeros_like(total_ref)
    elements(0, terms0, cells0)
    for i in range(HALF):
        expand(i, *even)
    elements(1, terms1, cells1)

    def two(i, carry):
        turn(jnp.minimum(2 * i + 2, BLOCKS - 1), even, odd)
        turn(jnp.minimum(2 * i + 3, BLOCKS - 1), odd, even)
        return carry

    lax.fori_loop(0, BLOCKS // 2, two, 0)

    span = VALS * FINE
    flat = total_ref[...].T
    total = jnp.concatenate([flat[0:span], flat[span : 2 * span]], 1)
    table.wait()
    mixed = jnp.dot(total.astype(jnp.bfloat16), first_ref[...], preferred_element_type=jnp.float32)
    ur = mixed[:, :XB].reshape(VALS, FINE, XB)
    ui = mixed[:, XB:].reshape(VALS, FINE, XB)
    wr, wi = twiddle_ref[0:FINE][None], twiddle_ref[FINE : 2 * FINE][None]
    vr = ur * wr - ui * wi
    vi = ur * wi + ui * wr
    middle = total[:, COARSE : COARSE + 1].reshape(VALS, FINE, 1)
    is_odd = lax.broadcasted_iota(jnp.int32, (1, 1, XB), 2) % 2 == 1
    flip = jnp.where(is_odd, -1.0, 1.0) * (1.0 / math.sqrt(VIS_ALL))
    at_zero = lax.broadcasted_iota(jnp.int32, (1, FINE, XB), 1) == 0
    vi = jnp.where(at_zero, middle * flip, vi)
    both = jnp.concatenate([vr.reshape(span, XB), vi.reshape(span, XB)], 0)
    image_ref[...] = jnp.dot(
        second_ref[...], both, preferred_element_type=jnp.float32, precision=lax.Precision.HIGHEST
    )
    size = TERMS * FINE
    for s, out in enumerate((o0, o1, o2, o3)):
        spot = (2, 3, 1, 0)[s]
        before = ((own ^ s) + FACETS - 1) % FACETS ^ own
        before = jnp.where(before < 2, before + 2, 3 - before)
        out[0:size] = image_ref[spot * size : (spot + 1) * size].astype(out.dtype)
        prior = image_ref[pl.ds(pl.multiple_of(before * size, 8), size), :]
        strips = [prior[term * FINE + FINE - 1 : term * FINE + FINE] for term in range(TERMS)]
        strips = jnp.concatenate(strips + [jnp.zeros((CHUNK - size - TERMS, XB), jnp.float32)], 0)
        out[size:CHUNK] = strips.astype(out.dtype)


def blend_kernel(place_ref, p0, p1, p2, p3, mask_ref, out_ref):
    size = TERMS * FINE
    image = p0[...]
    for part in (p1, p2, p3):
        image = image + part[...].astype(jnp.float32)
    strip = image[size : size + TERMS, XB - OVER :]
    has_left = (place_ref[0] > 0).astype(jnp.float32)
    pixel = lax.broadcasted_iota(jnp.int32, (1, OVER), 1).astype(jnp.float32)
    ramp = 1.0 - (pixel + 0.5) / OVER
    weight = mask_ref[0].astype(jnp.float32) * ramp * has_left
    for term in range(TERMS):
        for xa in range(FINE):
            line = image[term * FINE + xa : term * FINE + xa + 1]
            if xa == 0:
                head = line[:, :OVER]
                head = head + weight * (strip[term : term + 1] - head)
                out_ref[term, :, 0:OVER] = head
                out_ref[term, :, OVER:XB] = line[:, OVER:]
            else:
                out_ref[term, :, xa * XB : (xa + 1) * XB] = line


def swap_pairs():
    pairs = []
    for facet in range(FACETS):
        for z in range(SIDE):
            for y in range(SIDE):
                for x in range(SIDE):
                    here = y * SIDE + x
                    plane = (z + BEHIND[facet]) % SIDE
                    source = ((3 - facet) ^ (y & 1)) * IMG_ROWS + plane * BLOCKS + here
                    pairs.append((source, facet * IMG_ROWS + z * BLOCKS + here))
    return pairs


def per_device(visibilities, uv_coords, cells, centres, intersection_mask):
    vmem = pl.BlockSpec(memory_space=pltpu.VMEM)
    smem = pl.BlockSpec(memory_space=pltpu.SMEM)
    hbm = pl.BlockSpec(memory_space=pltpu.HBM)
    facet, spot = lax.axis_index("facet"), lax.axis_index("vis")
    place = jnp.stack([facet, spot]).astype(jnp.int32)
    given = (visibilities, uv_coords.T, cells, centres)
    given = [pltpu.with_memory_space_constraint(one, pltpu.HBM) for one in given]
    packed = pl.pallas_call(
        pack_kernel,
        out_shape=jax.ShapeDtypeStruct((PACKED, 2 * CH), jnp.bfloat16),
        in_specs=[hbm] * 4,
        out_specs=vmem,
        scratch_shapes=[pltpu.VMEM(one.shape, one.dtype) for one in given]
        + [pltpu.SemaphoreType.DMA((4,))],
        compiler_params=pltpu.CompilerParams(vmem_limit_bytes=2 << 20),
        name="pack",
    )(*given)
    packed = lax.ppermute(packed, ("facet", "vis"), swap_pairs())
    packed, centre = lax.optimization_barrier((packed, centres))
    pair = lax.ppermute(centre, "facet", [(i, i ^ 1) for i in range(FACETS)])
    planes = [[z * BLOCKS + i for i in range(BLOCKS)] for z in range(SIDE)]
    blocks = lax.all_to_all(
        pl.pallas_call(
            spread_kernel,
            out_shape=jax.ShapeDtypeStruct((BLOCKS,) + packed.shape, packed.dtype),
            in_specs=[vmem],
            out_specs=vmem,
            compiler_params=pltpu.CompilerParams(vmem_limit_bytes=2 << 20),
            name="spread",
        )(packed),
        "vis", 0, 0, axis_index_groups=planes,
    )
    first, twiddle, second = tables()
    first = pltpu.with_memory_space_constraint(first, pltpu.HBM)
    chunk = [
        jax.ShapeDtypeStruct((CHUNK, XB), jnp.bfloat16 if s else jnp.float32)
        for s in range(FACETS)
    ]
    span = 2 * VALS * FINE
    wide = ROWS * CH
    parts = pl.pallas_call(
        grid_kernel,
        out_shape=chunk,
        in_specs=[smem] + [vmem] * 3 + [hbm] + [vmem] * 2,
        out_specs=[vmem] * FACETS,
        scratch_shapes=[
            pltpu.VMEM((2 * VALS, HALF, 2 * CH), jnp.float32),
            pltpu.VMEM((2 * VALS, HALF, 2 * CH), jnp.float32),
            pltpu.VMEM((2, HALF, 2 * CH), jnp.float32),
            pltpu.VMEM((2, HALF, 2 * CH), jnp.float32),
            pltpu.VMEM((span, wide), jnp.bfloat16),
            pltpu.VMEM((span, wide), jnp.bfloat16),
            pltpu.VMEM((COARSE, wide), jnp.bfloat16),
            pltpu.VMEM((COARSE, wide), jnp.bfloat16),
            pltpu.VMEM((COARSE, span), jnp.float32),
            pltpu.VMEM((VALS * FINE, XB), jnp.float32),
            pltpu.VMEM((COARSE, 2 * CH), jnp.bfloat16),
            pltpu.VMEM((2 * COARSE, 2 * XB), jnp.bfloat16),
            pltpu.SemaphoreType.DMA,
        ],
        compiler_params=pltpu.CompilerParams(vmem_limit_bytes=40 << 20),
        name="grid",
    )(place, blocks, centres, pair, first, twiddle, second)
    got = [parts[0]]
    for s in range(1, FACETS):
        got.append(lax.ppermute(parts[s], "facet", [(i, i ^ s) for i in range(FACETS)]))
    return pl.pallas_call(
        blend_kernel,
        out_shape=jax.ShapeDtypeStruct((TERMS, 1, GRID), jnp.float32),
        in_specs=[smem] + [vmem] * 5,
        out_specs=vmem,
        compiler_params=pltpu.CompilerParams(vmem_limit_bytes=2 << 20),
        name="blend",
    )(place, *got, intersection_mask)


def solution(mesh):
    placed = (
        P("vis", None),
        P("vis", None),
        P(None, "vis", None),
        P("facet", None),
        P("facet", "vis", None),
    )
    return jax.shard_map(
        per_device, mesh=mesh, in_specs=placed, out_specs=P(None, "vis", "facet"), check_vma=False
    )
```

```python
import math

import jax
import jax.numpy as jnp
import numpy as np
from jax import lax
from jax.experimental import pallas as pl
from jax.experimental.pallas import tpu as pltpu
from jax.sharding import PartitionSpec as P

GRID = 4096
CH = 64
TERMS = 3
OVER = 256
FACETS = 4
VIS_ROWS = 2048
IMG_ROWS = 64
VIS_ALL = VIS_ROWS * CH
SIDE = 4
BLOCKS = SIDE * SIDE
ROWS = VIS_ROWS // IMG_ROWS
HALF = ROWS // 2
PACKED = 4 * HALF + 8
BEHIND = (0, -1, 1, 2)
FINE = 8
COARSE = GRID // 2 // FINE
XB = GRID // FINE
VALS = FACETS * TERMS
STEP = 2
CHUNK = 32

COS = (0.99999999, -19.73920447, 64.93911593, -85.45011343, 60.16742979, -25.96688461, 6.52770596)
SIN = (6.28318491, -41.3415883, 81.59991362, -76.6141403, 41.34136538, -12.46881862)


def tables():
    gh = np.arange(COARSE)[:, None]
    xb = np.arange(XB)[None, :]
    ang = 2 * np.pi * ((gh * xb) % XB) / XB
    cosine, sine = np.cos(ang), np.sin(ang)
    first = np.concatenate(
        [np.concatenate([cosine, sine], 1), np.concatenate([-sine, cosine], 1)], 0
    )
    gl = np.arange(FINE)[:, None]
    tw = 2 * np.pi * (gl * xb) / GRID
    scale = np.where(gl % 2 == 0, 1.0, -1.0) / math.sqrt(VIS_ALL)
    twiddle = np.concatenate([np.cos(tw) * scale, np.sin(tw) * scale], 0)
    xa = np.arange(FINE)[:, None]
    turn = 2 * np.pi * ((xa * np.arange(FINE)[None, :]) % FINE) / FINE
    real, imag = np.cos(turn), -np.sin(turn)
    imag[:, 0] = 1.0
    eye = np.eye(VALS)
    second = np.concatenate([np.kron(eye, real), np.kron(eye, imag)], 1)
    return (
        jnp.asarray(first, jnp.bfloat16),
        jnp.asarray(twiddle, jnp.float32),
        jnp.asarray(second, jnp.float32),
    )


def turns_cos_sin(turns):
    frac = turns - jnp.round(turns)
    sq = frac * frac
    cosine = jnp.full_like(sq, COS[-1])
    for coef in COS[-2::-1]:
        cosine = cosine * sq + coef
    sine = jnp.full_like(sq, SIN[-1])
    for coef in SIN[-2::-1]:
        sine = sine * sq + coef
    return cosine, sine * frac


def coded(cell):
    size = ((cell & 127) + 128) << ((cell >> 7) & 15)
    value = size.astype(jnp.float32)
    return jnp.where(cell >= GRID // 2, -value, value).astype(jnp.bfloat16)


def decoded(value):
    size = jnp.abs(value)
    high = jnp.where(value < 0.0, float(GRID // 2) - 128.0, -128.0)
    for step in (8, 4, 2, 1):
        over = size >= 128.0 * 2**step
        size = jnp.where(over, size * 2.0**-step, size)
        high = jnp.where(over, high + 128.0 * step, high)
    return size + high


def pack_kernel(
    vis_hbm, uv_hbm, cells_hbm, centre_hbm, out_ref, vis_ref, uv_ref, cells_ref, centre_ref, sems
):
    pairs = ((vis_hbm, vis_ref), (uv_hbm, uv_ref), (cells_hbm, cells_ref), (centre_hbm, centre_ref))
    copies = [pltpu.make_async_copy(a, b, sems.at[i]) for i, (a, b) in enumerate(pairs)]
    for copy in copies:
        copy.start()
    for copy in copies:
        copy.wait()
    lane = lax.broadcasted_iota(jnp.int32, (HALF, 2 * CH), 1)
    left = lane < CH
    vis = vis_ref[...].astype(jnp.float32)
    top, low = vis[:HALF], vis[HALF:]
    out_ref[0:16] = jnp.where(left, top, pltpu.roll(low, CH, 1)).astype(jnp.bfloat16)
    out_ref[16:32] = jnp.where(left, pltpu.roll(top, CH, 1), low).astype(jnp.bfloat16)
    for which in range(2):
        cells = cells_ref[which]
        both = jnp.concatenate([cells[:HALF], cells[HALF:]], 1)
        out_ref[32 + 16 * which : 48 + 16 * which] = coded(both)

    def pieces(value):
        high = value.astype(jnp.bfloat16).astype(jnp.float32)
        rest = value - high
        mid = rest.astype(jnp.bfloat16).astype(jnp.float32)
        return high, mid, rest - mid

    split = jnp.concatenate(pieces(uv_ref[...]), 0).astype(jnp.bfloat16)
    spots = lax.broadcasted_iota(jnp.int32, (6, 2 * CH), 0)
    spots = spots == lax.broadcasted_iota(jnp.int32, (6, 2 * CH), 1)
    columns = lax.dot_general(
        split, spots.astype(jnp.float32).astype(jnp.bfloat16), (((0,), (0,)), ((), ())),
        preferred_element_type=jnp.float32,
    )
    whole = columns[0:8]
    for i in (1, 2, 3):
        whole = whole + pltpu.roll(columns[8 * i : 8 * i + 8], 32 * i, 1)
    lane = lane[0:8]
    cen = jnp.where(lane % 2 == 0, centre_ref[0:1, 0:1], centre_ref[0:1, 1:2])
    for i, piece in enumerate(pieces(cen)):
        whole = jnp.where(lane // 2 == 3 + i, piece, whole)
    out_ref[64:72] = whole.astype(jnp.bfloat16)


def spread_kernel(block_ref, out_ref):
    for i in range(BLOCKS):
        out_ref[i] = block_ref[...]


def grid_kernel(
    place_ref, blocks_ref, own_ref, pair_ref, first_hbm, twiddle_ref, second_ref, o0, o1, o2, o3,
    terms0, terms1, cells0, cells1, total_ref, image_ref, iota_ref, first_ref, sem,
):
    table = pltpu.make_async_copy(first_hbm, first_ref, sem)
    table.start()
    own, row = place_ref[0], place_ref[1]
    lane = lax.broadcasted_iota(jnp.int32, (HALF, 2 * CH), 1)
    chan = (lane % CH).astype(jnp.float32)
    nu = (2.0 * chan + 1.0 - CH) / CH
    freq = 1.0 + 0.15 * nu
    nu2 = nu * nu
    step = (row - IMG_ROWS // 2).astype(jnp.float32) * (1.0 / GRID)
    count = lax.broadcasted_iota(jnp.int32, (COARSE, 2 * CH), 0)
    iota_ref[...] = count.astype(jnp.float32).astype(jnp.bfloat16)
    fine_iota = count[:FINE].astype(jnp.float32)
    one = jnp.ones((2 * FINE, 2 * CH), jnp.bfloat16)
    zero = jnp.zeros((2 * FINE, 2 * CH), jnp.bfloat16)

    def joined(section):
        return section + pltpu.roll(section, 2 * CH - 2, 1) + pltpu.roll(section, 2 * CH - 4, 1)

    cens = []
    for y in range(2):
        sect = joined(blocks_ref[y * SIDE, 64:72].astype(jnp.float32))
        cens.append((sect[0:1, 6:7], sect[0:1, 7:8]))
    for ref in (own_ref, pair_ref):
        cens.append((ref[0:1, 0:1], ref[0:1, 1:2]))

    def elements(block, terms_ref, cell_ref):
        def section(at):
            return blocks_ref[block, 16 * at : 16 * at + 16].astype(jnp.float32)

        real, imag = section(0), section(1)
        gr, gc = decoded(section(2)), decoded(section(3))
        place = joined(blocks_ref[block, 64:72].astype(jnp.float32))
        is_left = lane[0:8] < CH

        def column(at):
            both = [
                jnp.where(is_left, place[:, i : i + 1], place[:, CH + i : CH + i + 1])
                for i in (at, at + 32)
            ]
            return jnp.concatenate(both, 0)

        u, v = column(0), column(1)
        mid = (gc == float(GRID // 2)).astype(jnp.float32)
        folded = jnp.where(gc > GRID // 2, GRID - gc, gc * (1.0 - mid))
        sign = jnp.where(gc > GRID // 2, -1.0, jnp.where(folded == 0.0, 0.0, 1.0))
        cell = folded.astype(jnp.int32)
        cell_ref[0] = (cell & (FINE - 1)).astype(jnp.float32)
        cell_ref[1] = (cell >> (FINE.bit_length() - 1)).astype(jnp.float32)
        keep = 1.0 - mid
        ca, sa = turns_cos_sin(gr * step)
        for q in range(SIDE):
            proj = u * cens[q][0] + v * cens[q][1]
            cp, sp = turns_cos_sin(proj * freq)
            rr = (real * cp + imag * sp).astype(jnp.bfloat16).astype(jnp.float32)
            ri = (imag * cp - real * sp).astype(jnp.bfloat16).astype(jnp.float32)
            br = ca * rr - sa * ri
            bi = ca * ri + sa * rr
            bi = bi * sign + br * mid
            br = br * keep
            terms_ref[q] = br
            terms_ref[SIDE + q] = bi

    def expand(i, terms_ref, cell_ref):
        fine = jnp.broadcast_to(cell_ref[0, i : i + 1, :], (FINE, 2 * CH)) == fine_iota
        left = []
        for k in range(FACETS):
            terms = []
            for base in (2 * k, 2 * k + 1):
                base = jnp.broadcast_to(terms_ref[base, i : i + 1, :], (FINE, 2 * CH))
                base = jnp.where(fine, base, 0.0)
                terms += [base, base * nu[:FINE], base * nu2[:FINE]]
            left.append(jnp.concatenate(terms, 0).astype(jnp.bfloat16))
        coarse = jnp.broadcast_to(cell_ref[1, i : i + 1, :], (2 * FINE, 2 * CH))
        coarse = coarse.astype(jnp.bfloat16)
        right = [
            jnp.where(coarse == iota_ref[m * 2 * FINE : (m + 1) * 2 * FINE], one, zero)
            for m in range(COARSE // (2 * FINE))
        ]
        return jnp.concatenate(left, 0), jnp.concatenate(right, 0)

    def turn(block, here, ahead):
        part = total_ref[...]
        elements(block, ahead[0], ahead[1])
        for i in range(0, HALF, STEP):
            both = [expand(i + j, here[0], here[1]) for j in range(STEP)]
            left = jnp.concatenate([sides[0] for sides in both], 1)
            right = jnp.concatenate([sides[1] for sides in both], 1)
            part = part + lax.dot_general(
                right, left, (((1,), (1,)), ((), ())), preferred_element_type=jnp.float32
            )
        total_ref[...] = part

    even, odd = (terms0, cells0), (terms1, cells1)
    total_ref[...] = jnp.zeros_like(total_ref)
    elements(0, terms0, cells0)

    def two(i, carry):
        turn(2 * i + 1, even, odd)
        turn(jnp.minimum(2 * i + 2, BLOCKS - 1), odd, even)
        return carry

    lax.fori_loop(0, BLOCKS // 2, two, 0, unroll=4)

    span = VALS * FINE
    flat = total_ref[...].T
    total = jnp.concatenate([flat[0:span], flat[span : 2 * span]], 1)
    table.wait()
    mixed = jnp.dot(total.astype(jnp.bfloat16), first_ref[...], preferred_element_type=jnp.float32)
    ur = mixed[:, :XB].reshape(VALS, FINE, XB)
    ui = mixed[:, XB:].reshape(VALS, FINE, XB)
    wr, wi = twiddle_ref[0:FINE][None], twiddle_ref[FINE : 2 * FINE][None]
    vr = ur * wr - ui * wi
    vi = ur * wi + ui * wr
    middle = total[:, COARSE : COARSE + 1].reshape(VALS, FINE, 1)
    is_odd = lax.broadcasted_iota(jnp.int32, (1, 1, XB), 2) % 2 == 1
    flip = jnp.where(is_odd, -1.0, 1.0) * (1.0 / math.sqrt(VIS_ALL))
    at_zero = lax.broadcasted_iota(jnp.int32, (1, FINE, XB), 1) == 0
    vi = jnp.where(at_zero, middle * flip, vi)
    both = jnp.concatenate([vr.reshape(span, XB), vi.reshape(span, XB)], 0)
    image_ref[...] = jnp.dot(
        second_ref[...], both, preferred_element_type=jnp.float32, precision=lax.Precision.HIGHEST
    )
    size = TERMS * FINE
    for s, out in enumerate((o0, o1, o2, o3)):
        spot = (2, 3, 1, 0)[s]
        before = ((own ^ s) + FACETS - 1) % FACETS ^ own
        before = jnp.where(before < 2, before + 2, 3 - before)
        out[0:size] = image_ref[spot * size : (spot + 1) * size].astype(out.dtype)
        prior = image_ref[pl.ds(pl.multiple_of(before * size, 8), size), :]
        strips = [prior[term * FINE + FINE - 1 : term * FINE + FINE] for term in range(TERMS)]
        strips = jnp.concatenate(strips + [jnp.zeros((CHUNK - size - TERMS, XB), jnp.float32)], 0)
        out[size:CHUNK] = strips.astype(out.dtype)


def blend_kernel(place_ref, p0, p1, p2, p3, mask_ref, out_ref):
    size = TERMS * FINE
    image = p0[...]
    for part in (p1, p2, p3):
        image = image + part[...].astype(jnp.float32)
    strip = image[size : size + TERMS, XB - OVER :]
    has_left = (place_ref[0] > 0).astype(jnp.float32)
    pixel = lax.broadcasted_iota(jnp.int32, (1, OVER), 1).astype(jnp.float32)
    ramp = 1.0 - (pixel + 0.5) / OVER
    weight = mask_ref[0].astype(jnp.float32) * ramp * has_left
    for term in range(TERMS):
        for xa in range(FINE):
            line = image[term * FINE + xa : term * FINE + xa + 1]
            if xa == 0:
                head = line[:, :OVER]
                head = head + weight * (strip[term : term + 1] - head)
                out_ref[term, :, 0:OVER] = head
                out_ref[term, :, OVER:XB] = line[:, OVER:]
            else:
                out_ref[term, :, xa * XB : (xa + 1) * XB] = line


def swap_pairs():
    pairs = []
    for facet in range(FACETS):
        for z in range(SIDE):
            for y in range(SIDE):
                for x in range(SIDE):
                    here = y * SIDE + x
                    plane = (z + BEHIND[facet]) % SIDE
                    source = ((3 - facet) ^ (y & 1)) * IMG_ROWS + plane * BLOCKS + here
                    pairs.append((source, facet * IMG_ROWS + z * BLOCKS + here))
    return pairs


def partial_images(place, blocks, centres, pair):
    vmem = pl.BlockSpec(memory_space=pltpu.VMEM)
    smem = pl.BlockSpec(memory_space=pltpu.SMEM)
    hbm = pl.BlockSpec(memory_space=pltpu.HBM)
    first, twiddle, second = tables()
    first = pltpu.with_memory_space_constraint(first, pltpu.HBM)
    chunk = [
        jax.ShapeDtypeStruct((CHUNK, XB), jnp.bfloat16 if s else jnp.float32)
        for s in range(FACETS)
    ]
    span = 2 * VALS * FINE
    return pl.pallas_call(
        grid_kernel,
        out_shape=chunk,
        in_specs=[smem] + [vmem] * 3 + [hbm] + [vmem] * 2,
        out_specs=[vmem] * FACETS,
        scratch_shapes=[
            pltpu.VMEM((2 * FACETS, HALF, 2 * CH), jnp.float32),
            pltpu.VMEM((2 * FACETS, HALF, 2 * CH), jnp.float32),
            pltpu.VMEM((2, HALF, 2 * CH), jnp.float32),
            pltpu.VMEM((2, HALF, 2 * CH), jnp.float32),
            pltpu.VMEM((COARSE, span), jnp.float32),
            pltpu.VMEM((VALS * FINE, XB), jnp.float32),
            pltpu.VMEM((COARSE, 2 * CH), jnp.bfloat16),
            pltpu.VMEM((2 * COARSE, 2 * XB), jnp.bfloat16),
            pltpu.SemaphoreType.DMA,
        ],
        compiler_params=pltpu.CompilerParams(vmem_limit_bytes=16 << 20),
        name="grid",
    )(place, blocks, centres, pair, first, twiddle, second)


def per_device(visibilities, uv_coords, cells, centres, intersection_mask):
    vmem = pl.BlockSpec(memory_space=pltpu.VMEM)
    smem = pl.BlockSpec(memory_space=pltpu.SMEM)
    hbm = pl.BlockSpec(memory_space=pltpu.HBM)
    facet, spot = lax.axis_index("facet"), lax.axis_index("vis")
    place = jnp.stack([facet, spot]).astype(jnp.int32)
    given = (visibilities, uv_coords.T, cells, centres)
    given = [pltpu.with_memory_space_constraint(one, pltpu.HBM) for one in given]
    packed = pl.pallas_call(
        pack_kernel,
        out_shape=jax.ShapeDtypeStruct((PACKED, 2 * CH), jnp.bfloat16),
        in_specs=[hbm] * 4,
        out_specs=vmem,
        scratch_shapes=[pltpu.VMEM(one.shape, one.dtype) for one in given]
        + [pltpu.SemaphoreType.DMA((4,))],
        compiler_params=pltpu.CompilerParams(vmem_limit_bytes=2 << 20),
        name="pack",
    )(*given)
    packed = lax.ppermute(packed, ("facet", "vis"), swap_pairs())
    packed, centre = lax.optimization_barrier((packed, centres))
    pair = lax.ppermute(centre, "facet", [(i, i ^ 1) for i in range(FACETS)])
    planes = [[z * BLOCKS + i for i in range(BLOCKS)] for z in range(SIDE)]
    blocks = lax.all_to_all(
        pl.pallas_call(
            spread_kernel,
            out_shape=jax.ShapeDtypeStruct((BLOCKS,) + packed.shape, packed.dtype),
            in_specs=[vmem],
            out_specs=vmem,
            compiler_params=pltpu.CompilerParams(vmem_limit_bytes=2 << 20),
            name="spread",
        )(packed),
        "vis", 0, 0, axis_index_groups=planes,
    )
    parts = partial_images(place, blocks, centres, pair)
    got = [parts[0]]
    for s in range(1, FACETS):
        got.append(lax.ppermute(parts[s], "facet", [(i, i ^ s) for i in range(FACETS)]))
    return pl.pallas_call(
        blend_kernel,
        out_shape=jax.ShapeDtypeStruct((TERMS, 1, GRID), jnp.float32),
        in_specs=[smem] + [vmem] * 5,
        out_specs=vmem,
        compiler_params=pltpu.CompilerParams(vmem_limit_bytes=2 << 20),
        name="blend",
    )(place, *got, intersection_mask)


def solution(mesh):
    placed = (
        P("vis", None),
        P("vis", None),
        P(None, "vis", None),
        P("facet", None),
        P("facet", "vis", None),
    )
    return jax.shard_map(
        per_device, mesh=mesh, in_specs=placed, out_specs=P(None, "vis", "facet"), check_vma=False
    )
```

```python
import math

import jax
import jax.numpy as jnp
import ml_dtypes
import numpy as np
from jax import lax
from jax.experimental import pallas as pl
from jax.experimental.pallas import tpu as pltpu
from jax.sharding import PartitionSpec as P

GRID = 4096
CH = 64
TERMS = 3
OVER = 256
FACETS = 4
VIS_ROWS = 2048
IMG_ROWS = 64
VIS_ALL = VIS_ROWS * CH
SIDE = 4
BLOCKS = SIDE * SIDE
ROWS = VIS_ROWS // IMG_ROWS
HALF = ROWS // 2
PACKED = 4 * HALF + 8
BEHIND = (0, -1, 1, 2)
FINE = 8
COARSE = GRID // 2 // FINE
XB = GRID // FINE
VALS = FACETS * TERMS
STEP = 2
CHUNK = 32

COS = (0.99999999, -19.73920447, 64.93911593, -85.45011343, 60.16742979, -25.96688461, 6.52770596)
SIN = (6.28318491, -41.3415883, 81.59991362, -76.6141403, 41.34136538, -12.46881862)


def tables():
    gh = np.arange(COARSE)[:, None]
    xb = np.arange(XB)[None, :]
    ang = 2 * np.pi * ((gh * xb) % XB) / XB
    cosine, sine = np.cos(ang), np.sin(ang)
    first = np.concatenate(
        [np.concatenate([cosine, sine], 1), np.concatenate([-sine, cosine], 1)], 0
    )
    gl = np.arange(FINE)[:, None]
    tw = 2 * np.pi * (gl * xb) / GRID
    scale = np.where(gl % 2 == 0, 1.0, -1.0) / math.sqrt(VIS_ALL)
    twiddle = np.concatenate([np.cos(tw) * scale, np.sin(tw) * scale], 0)
    xa = np.arange(FINE)[:, None]
    turn = 2 * np.pi * ((xa * np.arange(FINE)[None, :]) % FINE) / FINE
    real, imag = np.cos(turn), -np.sin(turn)
    imag[:, 0] = 1.0
    eye = np.eye(VALS)
    second = np.concatenate([np.kron(eye, real), np.kron(eye, imag)], 1).astype(np.float32)
    second_high = second.astype(ml_dtypes.bfloat16)
    second_low = (second - second_high.astype(np.float32)).astype(ml_dtypes.bfloat16)
    return (
        jnp.asarray(first, jnp.bfloat16),
        jnp.asarray(twiddle, jnp.float32),
        (jnp.asarray(second_high), jnp.asarray(second_low)),
    )


def turns_cos_sin(turns):
    frac = turns - jnp.round(turns)
    sq = frac * frac
    cosine = jnp.full_like(sq, COS[-1])
    for coef in COS[-2::-1]:
        cosine = cosine * sq + coef
    sine = jnp.full_like(sq, SIN[-1])
    for coef in SIN[-2::-1]:
        sine = sine * sq + coef
    return cosine, sine * frac


def coded(cell):
    size = ((cell & 127) + 128) << ((cell >> 7) & 15)
    value = size.astype(jnp.float32)
    return jnp.where(cell >= GRID // 2, -value, value).astype(jnp.bfloat16)


def decoded(value):
    size = jnp.abs(value)
    high = jnp.where(value < 0.0, float(GRID // 2) - 128.0, -128.0)
    for step in (8, 4, 2, 1):
        over = size >= 128.0 * 2**step
        size = jnp.where(over, size * 2.0**-step, size)
        high = jnp.where(over, high + 128.0 * step, high)
    return size + high


def pack_kernel(
    vis_hbm, uv_hbm, cells_hbm, centre_hbm, out_ref, vis_ref, uv_ref, cells_ref, centre_ref, sems
):
    pairs = ((vis_hbm, vis_ref), (uv_hbm, uv_ref), (cells_hbm, cells_ref), (centre_hbm, centre_ref))
    copies = [pltpu.make_async_copy(a, b, sems.at[i]) for i, (a, b) in enumerate(pairs)]
    for copy in copies:
        copy.start()
    for copy in copies:
        copy.wait()
    lane = lax.broadcasted_iota(jnp.int32, (HALF, 2 * CH), 1)
    left = lane < CH
    vis = vis_ref[...].astype(jnp.float32)
    top, low = vis[:HALF], vis[HALF:]
    out_ref[0:16] = jnp.where(left, top, pltpu.roll(low, CH, 1)).astype(jnp.bfloat16)
    out_ref[16:32] = jnp.where(left, pltpu.roll(top, CH, 1), low).astype(jnp.bfloat16)
    for which in range(2):
        cells = cells_ref[which]
        both = jnp.concatenate([cells[:HALF], cells[HALF:]], 1)
        out_ref[32 + 16 * which : 48 + 16 * which] = coded(both)

    def pieces(value):
        high = value.astype(jnp.bfloat16).astype(jnp.float32)
        rest = value - high
        mid = rest.astype(jnp.bfloat16).astype(jnp.float32)
        return high, mid, rest - mid

    split = jnp.concatenate(pieces(uv_ref[...]), 0).astype(jnp.bfloat16)
    spots = lax.broadcasted_iota(jnp.int32, (6, 2 * CH), 0)
    spots = spots == lax.broadcasted_iota(jnp.int32, (6, 2 * CH), 1)
    columns = lax.dot_general(
        split, spots.astype(jnp.float32).astype(jnp.bfloat16), (((0,), (0,)), ((), ())),
        preferred_element_type=jnp.float32,
    )
    whole = columns[0:8]
    for i in (1, 2, 3):
        whole = whole + pltpu.roll(columns[8 * i : 8 * i + 8], 32 * i, 1)
    lane = lane[0:8]
    cen = jnp.where(lane % 2 == 0, centre_ref[0:1, 0:1], centre_ref[0:1, 1:2])
    for i, piece in enumerate(pieces(cen)):
        whole = jnp.where(lane // 2 == 3 + i, piece, whole)
    out_ref[64:72] = whole.astype(jnp.bfloat16)


def spread_kernel(block_ref, out_ref):
    for i in range(BLOCKS):
        out_ref[i] = block_ref[...]


def grid_kernel(
    blocks_ref, own_ref, pair_ref, first_hbm, twiddle_ref, high_ref, low_ref, o0, o1, o2, o3,
    terms0, terms1, cells0, cells1, total_ref, image_ref, iota_ref, first_ref, sem,
):
    table = pltpu.make_async_copy(first_hbm, first_ref, sem)
    table.start()
    own, row = lax.axis_index("facet"), lax.axis_index("vis")
    lane = lax.broadcasted_iota(jnp.int32, (HALF, 2 * CH), 1)
    chan = (lane % CH).astype(jnp.float32)
    nu = (2.0 * chan + 1.0 - CH) / CH
    freq = 1.0 + 0.15 * nu
    nu2 = nu * nu
    step = (row - IMG_ROWS // 2).astype(jnp.float32) * (1.0 / GRID)
    count = lax.broadcasted_iota(jnp.int32, (COARSE, 2 * CH), 0)
    iota_ref[...] = count.astype(jnp.float32).astype(jnp.bfloat16)
    fine_iota = count[:FINE].astype(jnp.float32)
    one = jnp.ones((2 * FINE, 2 * CH), jnp.bfloat16)
    zero = jnp.zeros((2 * FINE, 2 * CH), jnp.bfloat16)

    def joined(section):
        return section + pltpu.roll(section, 2 * CH - 2, 1) + pltpu.roll(section, 2 * CH - 4, 1)

    cens = []
    for y in range(2):
        sect = joined(blocks_ref[y * SIDE, 64:72].astype(jnp.float32))
        cens.append((sect[0:1, 6:7], sect[0:1, 7:8]))
    for ref in (own_ref, pair_ref):
        cens.append((ref[0:1, 0:1], ref[0:1, 1:2]))

    def elements(block, terms_ref, cell_ref):
        def section(at):
            return blocks_ref[block, 16 * at : 16 * at + 16].astype(jnp.float32)

        real, imag = section(0), section(1)
        gr, gc = decoded(section(2)), decoded(section(3))
        place = joined(blocks_ref[block, 64:72].astype(jnp.float32))
        is_left = lane[0:8] < CH

        def column(at):
            both = [
                jnp.where(is_left, place[:, i : i + 1], place[:, CH + i : CH + i + 1])
                for i in (at, at + 32)
            ]
            return jnp.concatenate(both, 0)

        u, v = column(0), column(1)
        mid = (gc == float(GRID // 2)).astype(jnp.float32)
        folded = jnp.where(gc > GRID // 2, GRID - gc, gc * (1.0 - mid))
        sign = jnp.where(gc > GRID // 2, -1.0, jnp.where(folded == 0.0, 0.0, 1.0))
        cell = folded.astype(jnp.int32)
        cell_ref[0] = (cell & (FINE - 1)).astype(jnp.float32)
        cell_ref[1] = (cell >> (FINE.bit_length() - 1)).astype(jnp.float32)
        keep = 1.0 - mid
        ca, sa = turns_cos_sin(gr * step)
        for q in range(SIDE):
            proj = u * cens[q][0] + v * cens[q][1]
            cp, sp = turns_cos_sin(proj * freq)
            rr = (real * cp + imag * sp).astype(jnp.bfloat16).astype(jnp.float32)
            ri = (imag * cp - real * sp).astype(jnp.bfloat16).astype(jnp.float32)
            br = ca * rr - sa * ri
            bi = ca * ri + sa * rr
            bi = bi * sign + br * mid
            br = br * keep
            terms_ref[q] = br
            terms_ref[SIDE + q] = bi

    def expand(i, terms_ref, cell_ref):
        fine = jnp.broadcast_to(cell_ref[0, i : i + 1, :], (FINE, 2 * CH)) == fine_iota
        left = []
        for k in range(FACETS):
            terms = []
            for base in (2 * k, 2 * k + 1):
                base = jnp.broadcast_to(terms_ref[base, i : i + 1, :], (FINE, 2 * CH))
                base = jnp.where(fine, base, 0.0)
                terms += [base, base * nu[:FINE], base * nu2[:FINE]]
            left.append(jnp.concatenate(terms, 0).astype(jnp.bfloat16))
        coarse = jnp.broadcast_to(cell_ref[1, i : i + 1, :], (2 * FINE, 2 * CH))
        coarse = coarse.astype(jnp.bfloat16)
        right = [
            jnp.where(coarse == iota_ref[m * 2 * FINE : (m + 1) * 2 * FINE], one, zero)
            for m in range(COARSE // (2 * FINE))
        ]
        return jnp.concatenate(left, 0), jnp.concatenate(right, 0)

    def turn(block, here, ahead):
        part = total_ref[...]
        elements(block, ahead[0], ahead[1])
        for i in range(0, HALF, STEP):
            both = [expand(i + j, here[0], here[1]) for j in range(STEP)]
            left = jnp.concatenate([sides[0] for sides in both], 1)
            right = jnp.concatenate([sides[1] for sides in both], 1)
            part = part + lax.dot_general(
                right, left, (((1,), (1,)), ((), ())), preferred_element_type=jnp.float32
            )
        total_ref[...] = part

    even, odd = (terms0, cells0), (terms1, cells1)
    total_ref[...] = jnp.zeros_like(total_ref)
    elements(0, terms0, cells0)

    def two(i, carry):
        turn(2 * i + 1, even, odd)
        turn(jnp.minimum(2 * i + 2, BLOCKS - 1), odd, even)
        return carry

    lax.fori_loop(0, BLOCKS // 2, two, 0, unroll=4)

    span = VALS * FINE
    flat = total_ref[...].T
    total = jnp.concatenate([flat[0:span], flat[span : 2 * span]], 1)
    table.wait()
    mixed = jnp.dot(total.astype(jnp.bfloat16), first_ref[...], preferred_element_type=jnp.float32)
    ur = mixed[:, :XB].reshape(VALS, FINE, XB)
    ui = mixed[:, XB:].reshape(VALS, FINE, XB)
    wr, wi = twiddle_ref[0:FINE][None], twiddle_ref[FINE : 2 * FINE][None]
    vr = ur * wr - ui * wi
    vi = ur * wi + ui * wr
    middle = total[:, COARSE : COARSE + 1].reshape(VALS, FINE, 1)
    is_odd = lax.broadcasted_iota(jnp.int32, (1, 1, XB), 2) % 2 == 1
    flip = jnp.where(is_odd, -1.0, 1.0) * (1.0 / math.sqrt(VIS_ALL))
    at_zero = lax.broadcasted_iota(jnp.int32, (1, FINE, XB), 1) == 0
    vi = jnp.where(at_zero, middle * flip, vi)
    both = jnp.concatenate([vr.reshape(span, XB), vi.reshape(span, XB)], 0)
    high = both.astype(jnp.bfloat16)
    low = (both - high.astype(jnp.float32)).astype(jnp.bfloat16)
    image = jnp.dot(high_ref[...], high, preferred_element_type=jnp.float32)
    image = image + jnp.dot(high_ref[...], low, preferred_element_type=jnp.float32)
    image = image + jnp.dot(low_ref[...], high, preferred_element_type=jnp.float32)
    image_ref[...] = image
    size = TERMS * FINE
    for s, out in enumerate((o0, o1, o2, o3)):
        spot = (2, 3, 1, 0)[s]
        before = ((own ^ s) + FACETS - 1) % FACETS ^ own
        before = jnp.where(before < 2, before + 2, 3 - before)
        out[0:size] = image_ref[spot * size : (spot + 1) * size].astype(out.dtype)
        prior = image_ref[pl.ds(pl.multiple_of(before * size, 8), size), :]
        strips = [prior[term * FINE + FINE - 1 : term * FINE + FINE] for term in range(TERMS)]
        strips = jnp.concatenate(strips + [jnp.zeros((CHUNK - size - TERMS, XB), jnp.float32)], 0)
        out[size:CHUNK] = strips.astype(out.dtype)


def blend_kernel(p0, p1, p2, p3, mask_ref, out_ref):
    size = TERMS * FINE
    image = p0[...]
    for part in (p1, p2, p3):
        image = image + part[...].astype(jnp.float32)
    strip = image[size : size + TERMS, XB - OVER :]
    has_left = (lax.axis_index("facet") > 0).astype(jnp.float32)
    pixel = lax.broadcasted_iota(jnp.int32, (1, OVER), 1).astype(jnp.float32)
    ramp = 1.0 - (pixel + 0.5) / OVER
    weight = mask_ref[0].astype(jnp.float32) * ramp * has_left
    for term in range(TERMS):
        for xa in range(FINE):
            line = image[term * FINE + xa : term * FINE + xa + 1]
            if xa == 0:
                head = line[:, :OVER]
                head = head + weight * (strip[term : term + 1] - head)
                out_ref[term, :, 0:OVER] = head
                out_ref[term, :, OVER:XB] = line[:, OVER:]
            else:
                out_ref[term, :, xa * XB : (xa + 1) * XB] = line


def swap_pairs():
    pairs = []
    for facet in range(FACETS):
        for z in range(SIDE):
            for y in range(SIDE):
                for x in range(SIDE):
                    here = y * SIDE + x
                    plane = (z + BEHIND[facet]) % SIDE
                    source = ((3 - facet) ^ (y & 1)) * IMG_ROWS + plane * BLOCKS + here
                    pairs.append((source, facet * IMG_ROWS + z * BLOCKS + here))
    return pairs


def partial_images(blocks, centres, pair):
    vmem = pl.BlockSpec(memory_space=pltpu.VMEM)
    hbm = pl.BlockSpec(memory_space=pltpu.HBM)
    first, twiddle, second = tables()
    first = pltpu.with_memory_space_constraint(first, pltpu.HBM)
    chunk = [
        jax.ShapeDtypeStruct((CHUNK, XB), jnp.bfloat16 if s else jnp.float32)
        for s in range(FACETS)
    ]
    span = 2 * VALS * FINE
    return pl.pallas_call(
        grid_kernel,
        out_shape=chunk,
        in_specs=[vmem] * 3 + [hbm] + [vmem] * 3,
        out_specs=[vmem] * FACETS,
        scratch_shapes=[
            pltpu.VMEM((2 * FACETS, HALF, 2 * CH), jnp.float32),
            pltpu.VMEM((2 * FACETS, HALF, 2 * CH), jnp.float32),
            pltpu.VMEM((2, HALF, 2 * CH), jnp.float32),
            pltpu.VMEM((2, HALF, 2 * CH), jnp.float32),
            pltpu.VMEM((COARSE, span), jnp.float32),
            pltpu.VMEM((VALS * FINE, XB), jnp.float32),
            pltpu.VMEM((COARSE, 2 * CH), jnp.bfloat16),
            pltpu.VMEM((2 * COARSE, 2 * XB), jnp.bfloat16),
            pltpu.SemaphoreType.DMA,
        ],
        compiler_params=pltpu.CompilerParams(vmem_limit_bytes=16 << 20),
        name="grid",
    )(blocks, centres, pair, first, twiddle, *second)


def per_device(visibilities, uv_coords, cells, centres, intersection_mask):
    vmem = pl.BlockSpec(memory_space=pltpu.VMEM)
    hbm = pl.BlockSpec(memory_space=pltpu.HBM)
    given = (visibilities, uv_coords.T, cells, centres)
    given = [pltpu.with_memory_space_constraint(one, pltpu.HBM) for one in given]
    packed = pl.pallas_call(
        pack_kernel,
        out_shape=jax.ShapeDtypeStruct((PACKED, 2 * CH), jnp.bfloat16),
        in_specs=[hbm] * 4,
        out_specs=vmem,
        scratch_shapes=[pltpu.VMEM(one.shape, one.dtype) for one in given]
        + [pltpu.SemaphoreType.DMA((4,))],
        compiler_params=pltpu.CompilerParams(vmem_limit_bytes=2 << 20),
        name="pack",
    )(*given)
    packed = lax.ppermute(packed, ("facet", "vis"), swap_pairs())
    packed, centre = lax.optimization_barrier((packed, centres))
    pair = lax.ppermute(centre, "facet", [(i, i ^ 1) for i in range(FACETS)])
    planes = [[z * BLOCKS + i for i in range(BLOCKS)] for z in range(SIDE)]
    blocks = lax.all_to_all(
        pl.pallas_call(
            spread_kernel,
            out_shape=jax.ShapeDtypeStruct((BLOCKS,) + packed.shape, packed.dtype),
            in_specs=[vmem],
            out_specs=vmem,
            compiler_params=pltpu.CompilerParams(vmem_limit_bytes=2 << 20),
            name="spread",
        )(packed),
        "vis", 0, 0, axis_index_groups=planes,
    )
    parts = partial_images(blocks, centres, pair)
    got = [parts[0]]
    for s in (2, 3, 1):
        got.append(lax.ppermute(parts[s], "facet", [(i, i ^ s) for i in range(FACETS)]))
    return pl.pallas_call(
        blend_kernel,
        out_shape=jax.ShapeDtypeStruct((TERMS, 1, GRID), jnp.float32),
        in_specs=[vmem] * 5,
        out_specs=vmem,
        compiler_params=pltpu.CompilerParams(vmem_limit_bytes=2 << 20),
        name="blend",
    )(*got, intersection_mask)


def solution(mesh):
    placed = (
        P("vis", None),
        P("vis", None),
        P(None, "vis", None),
        P("facet", None),
        P("facet", "vis", None),
    )
    return jax.shard_map(
        per_device, mesh=mesh, in_specs=placed, out_specs=P(None, "vis", "facet"), check_vma=False
    )
```

```python
import math

import jax
import jax.numpy as jnp
import ml_dtypes
import numpy as np
from jax import lax
from jax.experimental import pallas as pl
from jax.experimental.pallas import tpu as pltpu
from jax.sharding import PartitionSpec as P

GRID = 4096
CH = 64
TERMS = 3
OVER = 256
FACETS = 4
VIS_ROWS = 2048
IMG_ROWS = 64
VIS_ALL = VIS_ROWS * CH
SIDE = 4
BLOCKS = SIDE * SIDE
ROWS = VIS_ROWS // IMG_ROWS
HALF = ROWS // 2
PACKED = 4 * HALF + 8
BEHIND = (0, -1, 1, 2)
FINE = 8
COARSE = GRID // 2 // FINE
XB = GRID // FINE
VALS = FACETS * TERMS
STEP = 2
LANES = 128
CHUNK = 104

COS = (0.99999999, -19.73920447, 64.93911593, -85.45011343, 60.16742979, -25.96688461, 6.52770596)
SIN = (6.28318491, -41.3415883, 81.59991362, -76.6141403, 41.34136538, -12.46881862)


def tables():
    gh = np.arange(COARSE)[:, None]
    xb = np.arange(XB)[None, :]
    ang = 2 * np.pi * ((gh * xb) % XB) / XB
    cosine, sine = np.cos(ang), np.sin(ang)
    first = np.concatenate(
        [np.concatenate([cosine, sine], 1), np.concatenate([-sine, cosine], 1)], 0
    )
    gl = np.arange(FINE)[:, None]
    tw = 2 * np.pi * (gl * xb) / GRID
    scale = np.where(gl % 2 == 0, 1.0, -1.0) / math.sqrt(VIS_ALL)
    twiddle = np.concatenate([np.cos(tw) * scale, np.sin(tw) * scale], 0)
    xa = np.arange(FINE)[:, None]
    turn = 2 * np.pi * ((xa * np.arange(FINE)[None, :]) % FINE) / FINE
    real, imag = np.cos(turn), -np.sin(turn)
    imag[:, 0] = 1.0
    eye = np.eye(VALS)
    second = np.concatenate([np.kron(eye, real), np.kron(eye, imag)], 1).astype(np.float32)
    second_high = second.astype(ml_dtypes.bfloat16)
    second_low = (second - second_high.astype(np.float32)).astype(ml_dtypes.bfloat16)
    return (
        jnp.asarray(first, jnp.bfloat16),
        jnp.asarray(twiddle, jnp.float32),
        (jnp.asarray(second_high), jnp.asarray(second_low)),
    )


def turns_cos_sin(turns):
    frac = turns - jnp.round(turns)
    sq = frac * frac
    cosine = jnp.full_like(sq, COS[-1])
    for coef in COS[-2::-1]:
        cosine = cosine * sq + coef
    sine = jnp.full_like(sq, SIN[-1])
    for coef in SIN[-2::-1]:
        sine = sine * sq + coef
    return cosine, sine * frac


def coded(cell):
    size = ((cell & 127) + 128) << ((cell >> 7) & 15)
    value = size.astype(jnp.float32)
    return jnp.where(cell >= GRID // 2, -value, value).astype(jnp.bfloat16)


def decoded(value):
    size = jnp.abs(value)
    high = jnp.where(value < 0.0, float(GRID // 2) - 128.0, -128.0)
    for step in (8, 4, 2, 1):
        over = size >= 128.0 * 2**step
        size = jnp.where(over, size * 2.0**-step, size)
        high = jnp.where(over, high + 128.0 * step, high)
    return size + high


def pack_kernel(
    vis_hbm, uv_hbm, cells_hbm, centre_hbm, out_ref, copy_ref, vis_ref, uv_ref, cells_ref, centre_ref, sems
):
    pairs = ((vis_hbm, vis_ref), (uv_hbm, uv_ref), (cells_hbm, cells_ref), (centre_hbm, centre_ref))
    copies = [pltpu.make_async_copy(a, b, sems.at[i]) for i, (a, b) in enumerate(pairs)]
    for copy in copies:
        copy.start()
    for copy in copies:
        copy.wait()
    lane = lax.broadcasted_iota(jnp.int32, (HALF, 2 * CH), 1)
    left = lane < CH
    vis = vis_ref[...].astype(jnp.float32)
    top, low = vis[:HALF], vis[HALF:]
    out_ref[0:16] = jnp.where(left, top, pltpu.roll(low, CH, 1)).astype(jnp.bfloat16)
    out_ref[16:32] = jnp.where(left, pltpu.roll(top, CH, 1), low).astype(jnp.bfloat16)
    for which in range(2):
        cells = cells_ref[which]
        both = jnp.concatenate([cells[:HALF], cells[HALF:]], 1)
        out_ref[32 + 16 * which : 48 + 16 * which] = coded(both)

    def pieces(value):
        high = value.astype(jnp.bfloat16).astype(jnp.float32)
        rest = value - high
        mid = rest.astype(jnp.bfloat16).astype(jnp.float32)
        return high, mid, rest - mid

    split = jnp.concatenate(pieces(uv_ref[...]), 0).astype(jnp.bfloat16)
    spots = lax.broadcasted_iota(jnp.int32, (6, 2 * CH), 0)
    spots = spots == lax.broadcasted_iota(jnp.int32, (6, 2 * CH), 1)
    columns = lax.dot_general(
        split, spots.astype(jnp.float32).astype(jnp.bfloat16), (((0,), (0,)), ((), ())),
        preferred_element_type=jnp.float32,
    )
    whole = columns[0:8]
    for i in (1, 2, 3):
        whole = whole + pltpu.roll(columns[8 * i : 8 * i + 8], 32 * i, 1)
    lane = lane[0:8]
    cen = jnp.where(lane % 2 == 0, centre_ref[0:1, 0:1], centre_ref[0:1, 1:2])
    for i, piece in enumerate(pieces(cen)):
        whole = jnp.where(lane // 2 == 3 + i, piece, whole)
    out_ref[64:72] = whole.astype(jnp.bfloat16)
    copy_ref[...] = centre_ref[...]


def grid_kernel(
    blocks_ref, own_ref, pair_ref, first_hbm, twiddle_ref, high_ref, low_ref, o0, o1, o2, o3,
    terms0, terms1, cells0, cells1, total_ref, image_ref, iota_ref, first_ref, sem,
):
    table = pltpu.make_async_copy(first_hbm, first_ref, sem)
    table.start()
    own, row = lax.axis_index("facet"), lax.axis_index("vis")
    lane = lax.broadcasted_iota(jnp.int32, (HALF, 2 * CH), 1)
    chan = (lane % CH).astype(jnp.float32)
    nu = (2.0 * chan + 1.0 - CH) / CH
    freq = 1.0 + 0.15 * nu
    nu2 = nu * nu
    step = (row - IMG_ROWS // 2).astype(jnp.float32) * (1.0 / GRID)
    count = lax.broadcasted_iota(jnp.int32, (COARSE, 2 * CH), 0)
    iota_ref[...] = count.astype(jnp.float32).astype(jnp.bfloat16)
    fine_iota = count[:FINE].astype(jnp.float32)
    one = jnp.ones((2 * FINE, 2 * CH), jnp.bfloat16)
    zero = jnp.zeros((2 * FINE, 2 * CH), jnp.bfloat16)

    def joined(section):
        return section + pltpu.roll(section, 2 * CH - 2, 1) + pltpu.roll(section, 2 * CH - 4, 1)

    cens = []
    for y in range(2):
        sect = joined(blocks_ref[y * SIDE, 64:72].astype(jnp.float32))
        cens.append((sect[0:1, 6:7], sect[0:1, 7:8]))
    for ref in (own_ref, pair_ref):
        cens.append((ref[0:1, 0:1], ref[0:1, 1:2]))

    def elements(block, terms_ref, cell_ref):
        def section(at):
            return blocks_ref[block, 16 * at : 16 * at + 16].astype(jnp.float32)

        real, imag = section(0), section(1)
        gr, gc = decoded(section(2)), decoded(section(3))
        place = joined(blocks_ref[block, 64:72].astype(jnp.float32))
        is_left = lane[0:8] < CH

        def column(at):
            both = [
                jnp.where(is_left, place[:, i : i + 1], place[:, CH + i : CH + i + 1])
                for i in (at, at + 32)
            ]
            return jnp.concatenate(both, 0)

        u, v = column(0), column(1)
        mid = (gc == float(GRID // 2)).astype(jnp.float32)
        folded = jnp.where(gc > GRID // 2, GRID - gc, gc * (1.0 - mid))
        sign = jnp.where(gc > GRID // 2, -1.0, jnp.where(folded == 0.0, 0.0, 1.0))
        cell = folded.astype(jnp.int32)
        cell_ref[0] = (cell & (FINE - 1)).astype(jnp.float32)
        cell_ref[1] = (cell >> (FINE.bit_length() - 1)).astype(jnp.float32)
        keep = 1.0 - mid
        ca, sa = turns_cos_sin(gr * step)
        for q in range(SIDE):
            proj = u * cens[q][0] + v * cens[q][1]
            cp, sp = turns_cos_sin(proj * freq)
            rr = (real * cp + imag * sp).astype(jnp.bfloat16).astype(jnp.float32)
            ri = (imag * cp - real * sp).astype(jnp.bfloat16).astype(jnp.float32)
            br = ca * rr - sa * ri
            bi = ca * ri + sa * rr
            bi = bi * sign + br * mid
            br = br * keep
            terms_ref[q] = br
            terms_ref[SIDE + q] = bi

    def expand(i, terms_ref, cell_ref):
        fine = jnp.broadcast_to(cell_ref[0, i : i + 1, :], (FINE, 2 * CH)) == fine_iota
        left = []
        for k in range(FACETS):
            terms = []
            for base in (2 * k, 2 * k + 1):
                base = jnp.broadcast_to(terms_ref[base, i : i + 1, :], (FINE, 2 * CH))
                base = jnp.where(fine, base, 0.0)
                terms += [base, base * nu[:FINE], base * nu2[:FINE]]
            left.append(jnp.concatenate(terms, 0).astype(jnp.bfloat16))
        coarse = jnp.broadcast_to(cell_ref[1, i : i + 1, :], (2 * FINE, 2 * CH))
        coarse = coarse.astype(jnp.bfloat16)
        right = [
            jnp.where(coarse == iota_ref[m * 2 * FINE : (m + 1) * 2 * FINE], one, zero)
            for m in range(COARSE // (2 * FINE))
        ]
        return jnp.concatenate(left, 0), jnp.concatenate(right, 0)

    def turn(block, here, ahead):
        part = total_ref[...]
        elements(block, ahead[0], ahead[1])
        for i in range(0, HALF, STEP):
            both = [expand(i + j, here[0], here[1]) for j in range(STEP)]
            left = jnp.concatenate([sides[0] for sides in both], 1)
            right = jnp.concatenate([sides[1] for sides in both], 1)
            part = part + lax.dot_general(
                right, left, (((1,), (1,)), ((), ())), preferred_element_type=jnp.float32
            )
        total_ref[...] = part

    even, odd = (terms0, cells0), (terms1, cells1)
    total_ref[...] = jnp.zeros_like(total_ref)
    elements(0, terms0, cells0)

    def two(i, carry):
        turn(2 * i + 1, even, odd)
        turn(jnp.minimum(2 * i + 2, BLOCKS - 1), odd, even)
        return carry

    lax.fori_loop(0, BLOCKS // 2, two, 0, unroll=4)

    span = VALS * FINE
    flat = total_ref[...].T
    total = jnp.concatenate([flat[0:span], flat[span : 2 * span]], 1)
    table.wait()
    mixed = jnp.dot(total.astype(jnp.bfloat16), first_ref[...], preferred_element_type=jnp.float32)
    ur = mixed[:, :XB].reshape(VALS, FINE, XB)
    ui = mixed[:, XB:].reshape(VALS, FINE, XB)
    wr, wi = twiddle_ref[0:FINE][None], twiddle_ref[FINE : 2 * FINE][None]
    vr = ur * wr - ui * wi
    vi = ur * wi + ui * wr
    middle = total[:, COARSE : COARSE + 1].reshape(VALS, FINE, 1)
    is_odd = lax.broadcasted_iota(jnp.int32, (1, 1, XB), 2) % 2 == 1
    flip = jnp.where(is_odd, -1.0, 1.0) * (1.0 / math.sqrt(VIS_ALL))
    at_zero = lax.broadcasted_iota(jnp.int32, (1, FINE, XB), 1) == 0
    vi = jnp.where(at_zero, middle * flip, vi)
    both = jnp.concatenate([vr.reshape(span, XB), vi.reshape(span, XB)], 0)
    high = both.astype(jnp.bfloat16)
    low = (both - high.astype(jnp.float32)).astype(jnp.bfloat16)
    image = jnp.dot(high_ref[...], high, preferred_element_type=jnp.float32)
    image = image + jnp.dot(high_ref[...], low, preferred_element_type=jnp.float32)
    image = image + jnp.dot(low_ref[...], high, preferred_element_type=jnp.float32)
    image_ref[...] = image
    size = TERMS * FINE
    for s, out in enumerate((o0, o1, o2, o3)):
        spot = (2, 3, 1, 0)[s]
        before = ((own ^ s) + FACETS - 1) % FACETS ^ own
        before = jnp.where(before < 2, before + 2, 3 - before)
        mine = image_ref[spot * size : (spot + 1) * size]
        prior = image_ref[pl.ds(pl.multiple_of(before * size, 8), size), :]
        for c in range(XB // LANES):
            out[c * size : (c + 1) * size] = mine[:, c * LANES : (c + 1) * LANES].astype(out.dtype)
        strips = [
            prior[term * FINE + FINE - 1 : term * FINE + FINE, at : at + LANES]
            for at in range(XB - OVER, XB, LANES)
            for term in range(TERMS)
        ]
        strips = jnp.concatenate(strips + [jnp.zeros((2, LANES), jnp.float32)], 0)
        out[CHUNK - 8 : CHUNK] = strips.astype(out.dtype)


def blend_kernel(p0, p1, p2, p3, mask_ref, out_ref):
    size = TERMS * FINE
    image = p0[...]
    for part in (p1, p2, p3):
        image = image + part[...].astype(jnp.float32)
    has_left = (lax.axis_index("facet") > 0).astype(jnp.float32)
    pixel = lax.broadcasted_iota(jnp.int32, (1, OVER), 1).astype(jnp.float32)
    ramp = 1.0 - (pixel + 0.5) / OVER
    weight = mask_ref[0].astype(jnp.float32) * ramp * has_left
    for term in range(TERMS):
        for xa in range(FINE):
            for c in range(XB // LANES):
                row = c * size + term * FINE + xa
                line = image[row : row + 1]
                if xa == 0 and c < OVER // LANES:
                    at = CHUNK - 8 + c * TERMS + term
                    strip = image[at : at + 1]
                    line = line + weight[:, c * LANES : (c + 1) * LANES] * (strip - line)
                at = xa * XB + c * LANES
                out_ref[term, :, at : at + LANES] = line


def swap_pairs():
    pairs = []
    for facet in range(FACETS):
        for z in range(SIDE):
            for y in range(SIDE):
                for x in range(SIDE):
                    here = y * SIDE + x
                    plane = (z + BEHIND[facet]) % SIDE
                    source = ((3 - facet) ^ (y & 1)) * IMG_ROWS + plane * BLOCKS + here
                    pairs.append((source, facet * IMG_ROWS + z * BLOCKS + here))
    return pairs


def partial_images(blocks, centres, pair):
    vmem = pl.BlockSpec(memory_space=pltpu.VMEM)
    hbm = pl.BlockSpec(memory_space=pltpu.HBM)
    first, twiddle, second = tables()
    first = pltpu.with_memory_space_constraint(first, pltpu.HBM)
    chunk = [
        jax.ShapeDtypeStruct((CHUNK, LANES), jnp.bfloat16 if s else jnp.float32)
        for s in range(FACETS)
    ]
    span = 2 * VALS * FINE
    return pl.pallas_call(
        grid_kernel,
        out_shape=chunk,
        in_specs=[vmem] * 3 + [hbm] + [vmem] * 3,
        out_specs=[vmem] * FACETS,
        scratch_shapes=[
            pltpu.VMEM((2 * FACETS, HALF, 2 * CH), jnp.float32),
            pltpu.VMEM((2 * FACETS, HALF, 2 * CH), jnp.float32),
            pltpu.VMEM((2, HALF, 2 * CH), jnp.float32),
            pltpu.VMEM((2, HALF, 2 * CH), jnp.float32),
            pltpu.VMEM((COARSE, span), jnp.float32),
            pltpu.VMEM((VALS * FINE, XB), jnp.float32),
            pltpu.VMEM((COARSE, 2 * CH), jnp.bfloat16),
            pltpu.VMEM((2 * COARSE, 2 * XB), jnp.bfloat16),
            pltpu.SemaphoreType.DMA,
        ],
        compiler_params=pltpu.CompilerParams(vmem_limit_bytes=16 << 20),
        name="grid",
    )(blocks, centres, pair, first, twiddle, *second)


def per_device(visibilities, uv_coords, cells, centres, intersection_mask):
    vmem = pl.BlockSpec(memory_space=pltpu.VMEM)
    hbm = pl.BlockSpec(memory_space=pltpu.HBM)
    given = (visibilities, uv_coords.T, cells, centres)
    given = [pltpu.with_memory_space_constraint(one, pltpu.HBM) for one in given]
    packed, centre = pl.pallas_call(
        pack_kernel,
        out_shape=[
            jax.ShapeDtypeStruct((PACKED, 2 * CH), jnp.bfloat16),
            jax.ShapeDtypeStruct((1, 2), jnp.float32),
        ],
        in_specs=[hbm] * 4,
        out_specs=[vmem] * 2,
        scratch_shapes=[pltpu.VMEM(one.shape, one.dtype) for one in given]
        + [pltpu.SemaphoreType.DMA((4,))],
        compiler_params=pltpu.CompilerParams(vmem_limit_bytes=2 << 20),
        name="pack",
    )(*given)
    pair = lax.ppermute(centre, "facet", [(i, i ^ 1) for i in range(FACETS)])
    packed = lax.ppermute(packed, ("facet", "vis"), swap_pairs())
    packed, pair = lax.optimization_barrier((packed, pair))
    planes = [[z * BLOCKS + i for i in range(BLOCKS)] for z in range(SIDE)]
    blocks = lax.all_to_all(
        jnp.broadcast_to(packed[None], (BLOCKS,) + packed.shape),
        "vis", 0, 0, axis_index_groups=planes,
    )
    parts = partial_images(blocks, centre, pair)
    got = [parts[0]]
    for s in (2, 3, 1):
        got.append(lax.ppermute(parts[s], "facet", [(i, i ^ s) for i in range(FACETS)]))
    return pl.pallas_call(
        blend_kernel,
        out_shape=jax.ShapeDtypeStruct((TERMS, 1, GRID), jnp.float32),
        in_specs=[vmem] * 5,
        out_specs=vmem,
        compiler_params=pltpu.CompilerParams(vmem_limit_bytes=2 << 20),
        name="blend",
    )(*got, intersection_mask)


def solution(mesh):
    placed = (
        P("vis", None),
        P("vis", None),
        P(None, "vis", None),
        P("facet", None),
        P("facet", "vis", None),
    )
    return jax.shard_map(
        per_device, mesh=mesh, in_specs=placed, out_specs=P(None, "vis", "facet"), check_vma=False
    )
```

```python
import math

import jax
import jax.numpy as jnp
import ml_dtypes
import numpy as np
from jax import lax
from jax.experimental import pallas as pl
from jax.experimental.pallas import tpu as pltpu
from jax.sharding import PartitionSpec as P

GRID = 4096
CH = 64
TERMS = 3
OVER = 256
FACETS = 4
VIS_ROWS = 2048
IMG_ROWS = 64
VIS_ALL = VIS_ROWS * CH
SIDE = 4
BLOCKS = SIDE * SIDE
ROWS = VIS_ROWS // IMG_ROWS
HALF = ROWS // 2
PACKED = 4 * HALF + 8
BEHIND = (0, -1, 1, 2)
FINE = 8
COARSE = GRID // 2 // FINE
XB = GRID // FINE
VALS = FACETS * TERMS
STEP = 2
LANES = 128
CHUNK = 104

COS = (0.99999999, -19.73920447, 64.93911593, -85.45011343, 60.16742979, -25.96688461, 6.52770596)
SIN = (6.28318491, -41.3415883, 81.59991362, -76.6141403, 41.34136538, -12.46881862)


def tables():
    gh = np.arange(COARSE)[:, None]
    xb = np.arange(XB)[None, :]
    ang = 2 * np.pi * ((gh * xb) % XB) / XB
    cosine, sine = np.cos(ang), np.sin(ang)
    first = np.concatenate(
        [np.concatenate([cosine, sine], 1), np.concatenate([-sine, cosine], 1)], 0
    )
    gl = np.arange(FINE)[:, None]
    tw = 2 * np.pi * (gl * xb) / GRID
    scale = np.where(gl % 2 == 0, 1.0, -1.0) / math.sqrt(VIS_ALL)
    twiddle = np.concatenate([np.cos(tw) * scale, np.sin(tw) * scale], 0)
    xa = np.arange(FINE)[:, None]
    turn = 2 * np.pi * ((xa * np.arange(FINE)[None, :]) % FINE) / FINE
    real, imag = np.cos(turn), -np.sin(turn)
    imag[:, 0] = 1.0
    eye = np.eye(VALS)
    second = np.concatenate([np.kron(eye, real), np.kron(eye, imag)], 1).astype(np.float32)
    second_high = second.astype(ml_dtypes.bfloat16)
    second_low = (second - second_high.astype(np.float32)).astype(ml_dtypes.bfloat16)
    return (
        jnp.asarray(first, jnp.bfloat16),
        jnp.asarray(twiddle, jnp.float32),
        (jnp.asarray(second_high), jnp.asarray(second_low)),
    )


def turns_cos_sin(turns):
    frac = turns - jnp.round(turns)
    sq = frac * frac
    cosine = jnp.full_like(sq, COS[-1])
    for coef in COS[-2::-1]:
        cosine = cosine * sq + coef
    sine = jnp.full_like(sq, SIN[-1])
    for coef in SIN[-2::-1]:
        sine = sine * sq + coef
    return cosine, sine * frac


def coded(cell):
    size = ((cell & 127) + 128) << ((cell >> 7) & 15)
    value = size.astype(jnp.float32)
    return jnp.where(cell >= GRID // 2, -value, value).astype(jnp.bfloat16)


def decoded(value):
    size = jnp.abs(value)
    high = jnp.where(value < 0.0, float(GRID // 2) - 128.0, -128.0)
    for step in (8, 4, 2, 1):
        over = size >= 128.0 * 2**step
        size = jnp.where(over, size * 2.0**-step, size)
        high = jnp.where(over, high + 128.0 * step, high)
    return size + high


def pack_kernel(
    vis_hbm, uv_hbm, cells_hbm, centre_hbm, out_ref, copy_ref, vis_ref, uv_ref, cells_ref, centre_ref, sems
):
    pairs = ((vis_hbm, vis_ref), (uv_hbm, uv_ref), (cells_hbm, cells_ref), (centre_hbm, centre_ref))
    copies = [pltpu.make_async_copy(a, b, sems.at[i]) for i, (a, b) in enumerate(pairs)]
    for i in (1, 3, 0, 2):
        copies[i].start()
    copies[1].wait()
    copies[3].wait()
    lane = lax.broadcasted_iota(jnp.int32, (HALF, 2 * CH), 1)

    def pieces(value):
        high = value.astype(jnp.bfloat16).astype(jnp.float32)
        rest = value - high
        mid = rest.astype(jnp.bfloat16).astype(jnp.float32)
        return high, mid, rest - mid

    split = jnp.concatenate(pieces(uv_ref[...]), 0).astype(jnp.bfloat16)
    spots = lax.broadcasted_iota(jnp.int32, (6, 2 * CH), 0)
    spots = spots == lax.broadcasted_iota(jnp.int32, (6, 2 * CH), 1)
    columns = lax.dot_general(
        split, spots.astype(jnp.float32).astype(jnp.bfloat16), (((0,), (0,)), ((), ())),
        preferred_element_type=jnp.float32,
    )
    whole = columns[0:8]
    for i in (1, 2, 3):
        whole = whole + pltpu.roll(columns[8 * i : 8 * i + 8], 32 * i, 1)
    cen = jnp.where(lane[0:8] % 2 == 0, centre_ref[0:1, 0:1], centre_ref[0:1, 1:2])
    for i, piece in enumerate(pieces(cen)):
        whole = jnp.where(lane[0:8] // 2 == 3 + i, piece, whole)
    out_ref[64:72] = whole.astype(jnp.bfloat16)
    copy_ref[...] = centre_ref[...]

    copies[0].wait()
    copies[2].wait()
    left = lane < CH
    vis = vis_ref[...].astype(jnp.float32)
    top, low = vis[:HALF], vis[HALF:]
    out_ref[0:16] = jnp.where(left, top, pltpu.roll(low, CH, 1)).astype(jnp.bfloat16)
    out_ref[16:32] = jnp.where(left, pltpu.roll(top, CH, 1), low).astype(jnp.bfloat16)
    for which in range(2):
        cells = cells_ref[which]
        both = jnp.concatenate([cells[:HALF], cells[HALF:]], 1)
        out_ref[32 + 16 * which : 48 + 16 * which] = coded(both)


def grid_kernel(
    blocks_ref, own_ref, pair_ref, first_hbm, twiddle_ref, high_ref, low_ref, o0, o1, o2, o3,
    terms0, terms1, cells0, cells1, total_ref, image_ref, iota_ref, first_ref, sem,
):
    table = pltpu.make_async_copy(first_hbm, first_ref, sem)
    table.start()
    own, row = lax.axis_index("facet"), lax.axis_index("vis")
    lane = lax.broadcasted_iota(jnp.int32, (HALF, 2 * CH), 1)
    chan = (lane % CH).astype(jnp.float32)
    nu = (2.0 * chan + 1.0 - CH) / CH
    freq = 1.0 + 0.15 * nu
    nu2 = nu * nu
    step = (row - IMG_ROWS // 2).astype(jnp.float32) * (1.0 / GRID)
    count = lax.broadcasted_iota(jnp.int32, (COARSE, 2 * CH), 0)
    iota_ref[...] = count.astype(jnp.float32).astype(jnp.bfloat16)
    fine_iota = count[:FINE].astype(jnp.float32)
    one = jnp.ones((2 * FINE, 2 * CH), jnp.bfloat16)
    zero = jnp.zeros((2 * FINE, 2 * CH), jnp.bfloat16)

    def joined(section):
        return section + pltpu.roll(section, 2 * CH - 2, 1) + pltpu.roll(section, 2 * CH - 4, 1)

    cens = []
    for y in range(2):
        sect = joined(blocks_ref[y * SIDE, 64:72].astype(jnp.float32))
        cens.append((sect[0:1, 6:7], sect[0:1, 7:8]))
    for ref in (own_ref, pair_ref):
        cens.append((ref[0:1, 0:1], ref[0:1, 1:2]))

    def elements(block, terms_ref, cell_ref):
        def section(at):
            return blocks_ref[block, 16 * at : 16 * at + 16].astype(jnp.float32)

        real, imag = section(0), section(1)
        gr, gc = decoded(section(2)), decoded(section(3))
        place = joined(blocks_ref[block, 64:72].astype(jnp.float32))
        is_left = lane[0:8] < CH

        def column(at):
            both = [
                jnp.where(is_left, place[:, i : i + 1], place[:, CH + i : CH + i + 1])
                for i in (at, at + 32)
            ]
            return jnp.concatenate(both, 0)

        u, v = column(0), column(1)
        mid = (gc == float(GRID // 2)).astype(jnp.float32)
        folded = jnp.where(gc > GRID // 2, GRID - gc, gc * (1.0 - mid))
        sign = jnp.where(gc > GRID // 2, -1.0, jnp.where(folded == 0.0, 0.0, 1.0))
        cell = folded.astype(jnp.int32)
        cell_ref[0] = (cell & (FINE - 1)).astype(jnp.float32)
        cell_ref[1] = (cell >> (FINE.bit_length() - 1)).astype(jnp.float32)
        keep = 1.0 - mid
        ca, sa = turns_cos_sin(gr * step)
        for q in range(SIDE):
            proj = u * cens[q][0] + v * cens[q][1]
            cp, sp = turns_cos_sin(proj * freq)
            rr = (real * cp + imag * sp).astype(jnp.bfloat16).astype(jnp.float32)
            ri = (imag * cp - real * sp).astype(jnp.bfloat16).astype(jnp.float32)
            br = ca * rr - sa * ri
            bi = ca * ri + sa * rr
            bi = bi * sign + br * mid
            br = br * keep
            terms_ref[q] = br
            terms_ref[SIDE + q] = bi

    def expand(i, terms_ref, cell_ref):
        fine = jnp.broadcast_to(cell_ref[0, i : i + 1, :], (FINE, 2 * CH)) == fine_iota
        left = []
        for k in range(FACETS):
            terms = []
            for base in (2 * k, 2 * k + 1):
                base = jnp.broadcast_to(terms_ref[base, i : i + 1, :], (FINE, 2 * CH))
                base = jnp.where(fine, base, 0.0)
                terms += [base, base * nu[:FINE], base * nu2[:FINE]]
            left.append(jnp.concatenate(terms, 0).astype(jnp.bfloat16))
        coarse = jnp.broadcast_to(cell_ref[1, i : i + 1, :], (2 * FINE, 2 * CH))
        coarse = coarse.astype(jnp.bfloat16)
        right = [
            jnp.where(coarse == iota_ref[m * 2 * FINE : (m + 1) * 2 * FINE], one, zero)
            for m in range(COARSE // (2 * FINE))
        ]
        return jnp.concatenate(left, 0), jnp.concatenate(right, 0)

    def turn(block, here, ahead):
        part = total_ref[...]
        elements(block, ahead[0], ahead[1])
        for i in range(0, HALF, STEP):
            both = [expand(i + j, here[0], here[1]) for j in range(STEP)]
            left = jnp.concatenate([sides[0] for sides in both], 1)
            right = jnp.concatenate([sides[1] for sides in both], 1)
            part = part + lax.dot_general(
                right, left, (((1,), (1,)), ((), ())), preferred_element_type=jnp.float32
            )
        total_ref[...] = part

    even, odd = (terms0, cells0), (terms1, cells1)
    total_ref[...] = jnp.zeros_like(total_ref)
    elements(0, terms0, cells0)

    def two(i, carry):
        turn(2 * i + 1, even, odd)
        turn(jnp.minimum(2 * i + 2, BLOCKS - 1), odd, even)
        return carry

    lax.fori_loop(0, BLOCKS // 2, two, 0, unroll=4)

    span = VALS * FINE
    flat = total_ref[...].T
    total = jnp.concatenate([flat[0:span], flat[span : 2 * span]], 1)
    table.wait()
    mixed = jnp.dot(total.astype(jnp.bfloat16), first_ref[...], preferred_element_type=jnp.float32)
    ur = mixed[:, :XB].reshape(VALS, FINE, XB)
    ui = mixed[:, XB:].reshape(VALS, FINE, XB)
    wr, wi = twiddle_ref[0:FINE][None], twiddle_ref[FINE : 2 * FINE][None]
    vr = ur * wr - ui * wi
    vi = ur * wi + ui * wr
    middle = total[:, COARSE : COARSE + 1].reshape(VALS, FINE, 1)
    is_odd = lax.broadcasted_iota(jnp.int32, (1, 1, XB), 2) % 2 == 1
    flip = jnp.where(is_odd, -1.0, 1.0) * (1.0 / math.sqrt(VIS_ALL))
    at_zero = lax.broadcasted_iota(jnp.int32, (1, FINE, XB), 1) == 0
    vi = jnp.where(at_zero, middle * flip, vi)
    both = jnp.concatenate([vr.reshape(span, XB), vi.reshape(span, XB)], 0)
    high = both.astype(jnp.bfloat16)
    low = (both - high.astype(jnp.float32)).astype(jnp.bfloat16)
    image = jnp.dot(high_ref[...], high, preferred_element_type=jnp.float32)
    image = image + jnp.dot(high_ref[...], low, preferred_element_type=jnp.float32)
    image = image + jnp.dot(low_ref[...], high, preferred_element_type=jnp.float32)
    image_ref[...] = image
    size = TERMS * FINE
    for s, out in enumerate((o0, o1, o2, o3)):
        spot = (2, 3, 1, 0)[s]
        before = ((own ^ s) + FACETS - 1) % FACETS ^ own
        before = jnp.where(before < 2, before + 2, 3 - before)
        mine = image_ref[spot * size : (spot + 1) * size]
        prior = image_ref[pl.ds(pl.multiple_of(before * size, 8), size), :]
        for c in range(XB // LANES):
            out[c * size : (c + 1) * size] = mine[:, c * LANES : (c + 1) * LANES].astype(out.dtype)
        strips = [
            prior[term * FINE + FINE - 1 : term * FINE + FINE, at : at + LANES]
            for at in range(XB - OVER, XB, LANES)
            for term in range(TERMS)
        ]
        strips = jnp.concatenate(strips + [jnp.zeros((2, LANES), jnp.float32)], 0)
        out[CHUNK - 8 : CHUNK] = strips.astype(out.dtype)


def blend_kernel(p0, p1, p2, p3, mask_ref, out_ref):
    size = TERMS * FINE
    image = p0[...]
    for part in (p1, p2, p3):
        image = image + part[...].astype(jnp.float32)
    has_left = (lax.axis_index("facet") > 0).astype(jnp.float32)
    pixel = lax.broadcasted_iota(jnp.int32, (1, OVER), 1).astype(jnp.float32)
    ramp = 1.0 - (pixel + 0.5) / OVER
    weight = mask_ref[0].astype(jnp.float32) * ramp * has_left
    for term in range(TERMS):
        for xa in range(FINE):
            for c in range(XB // LANES):
                row = c * size + term * FINE + xa
                line = image[row : row + 1]
                if xa == 0 and c < OVER // LANES:
                    at = CHUNK - 8 + c * TERMS + term
                    strip = image[at : at + 1]
                    line = line + weight[:, c * LANES : (c + 1) * LANES] * (strip - line)
                at = xa * XB + c * LANES
                out_ref[term, :, at : at + LANES] = line


def swap_pairs():
    pairs = []
    for facet in range(FACETS):
        for z in range(SIDE):
            for y in range(SIDE):
                for x in range(SIDE):
                    here = y * SIDE + x
                    plane = (z + BEHIND[facet]) % SIDE
                    source = ((3 - facet) ^ (y & 1)) * IMG_ROWS + plane * BLOCKS + here
                    pairs.append((source, facet * IMG_ROWS + z * BLOCKS + here))
    return pairs


def partial_images(blocks, centres, pair):
    vmem = pl.BlockSpec(memory_space=pltpu.VMEM)
    hbm = pl.BlockSpec(memory_space=pltpu.HBM)
    first, twiddle, second = tables()
    first = pltpu.with_memory_space_constraint(first, pltpu.HBM)
    chunk = [
        jax.ShapeDtypeStruct((CHUNK, LANES), jnp.bfloat16 if s else jnp.float32)
        for s in range(FACETS)
    ]
    span = 2 * VALS * FINE
    return pl.pallas_call(
        grid_kernel,
        out_shape=chunk,
        in_specs=[vmem] * 3 + [hbm] + [vmem] * 3,
        out_specs=[vmem] * FACETS,
        scratch_shapes=[
            pltpu.VMEM((2 * FACETS, HALF, 2 * CH), jnp.float32),
            pltpu.VMEM((2 * FACETS, HALF, 2 * CH), jnp.float32),
            pltpu.VMEM((2, HALF, 2 * CH), jnp.float32),
            pltpu.VMEM((2, HALF, 2 * CH), jnp.float32),
            pltpu.VMEM((COARSE, span), jnp.float32),
            pltpu.VMEM((VALS * FINE, XB), jnp.float32),
            pltpu.VMEM((COARSE, 2 * CH), jnp.bfloat16),
            pltpu.VMEM((2 * COARSE, 2 * XB), jnp.bfloat16),
            pltpu.SemaphoreType.DMA,
        ],
        compiler_params=pltpu.CompilerParams(vmem_limit_bytes=16 << 20),
        name="grid",
    )(blocks, centres, pair, first, twiddle, *second)


def per_device(visibilities, uv_coords, cells, centres, intersection_mask):
    vmem = pl.BlockSpec(memory_space=pltpu.VMEM)
    hbm = pl.BlockSpec(memory_space=pltpu.HBM)
    given = (visibilities, uv_coords.T, cells, centres)
    given = [pltpu.with_memory_space_constraint(one, pltpu.HBM) for one in given]
    packed, centre = pl.pallas_call(
        pack_kernel,
        out_shape=[
            jax.ShapeDtypeStruct((PACKED, 2 * CH), jnp.bfloat16),
            jax.ShapeDtypeStruct((1, 2), jnp.float32),
        ],
        in_specs=[hbm] * 4,
        out_specs=[vmem] * 2,
        scratch_shapes=[pltpu.VMEM(one.shape, one.dtype) for one in given]
        + [pltpu.SemaphoreType.DMA((4,))],
        compiler_params=pltpu.CompilerParams(vmem_limit_bytes=2 << 20),
        name="pack",
    )(*given)
    pair = lax.ppermute(centre, "facet", [(i, i ^ 1) for i in range(FACETS)])
    packed = lax.ppermute(packed, ("facet", "vis"), swap_pairs())
    packed, pair = lax.optimization_barrier((packed, pair))
    planes = [[z * BLOCKS + i for i in range(BLOCKS)] for z in range(SIDE)]
    blocks = lax.all_to_all(
        jnp.broadcast_to(packed[None], (BLOCKS,) + packed.shape),
        "vis", 0, 0, axis_index_groups=planes,
    )
    parts = partial_images(blocks, centre, pair)
    got = [parts[0]]
    for s in (3, 2, 1):
        got.append(lax.ppermute(parts[s], "facet", [(i, i ^ s) for i in range(FACETS)]))
    return pl.pallas_call(
        blend_kernel,
        out_shape=jax.ShapeDtypeStruct((TERMS, 1, GRID), jnp.float32),
        in_specs=[vmem] * 5,
        out_specs=vmem,
        compiler_params=pltpu.CompilerParams(vmem_limit_bytes=2 << 20),
        name="blend",
    )(*got, intersection_mask)


def solution(mesh):
    placed = (
        P("vis", None),
        P("vis", None),
        P(None, "vis", None),
        P("facet", None),
        P("facet", "vis", None),
    )
    return jax.shard_map(
        per_device, mesh=mesh, in_specs=placed, out_specs=P(None, "vis", "facet"), check_vma=False
    )
```

```python
import math

import jax
import jax.numpy as jnp
import ml_dtypes
import numpy as np
from jax import lax
from jax.experimental import pallas as pl
from jax.experimental.pallas import tpu as pltpu
from jax.sharding import PartitionSpec as P

GRID = 4096
CH = 64
TERMS = 3
OVER = 256
FACETS = 4
VIS_ROWS = 2048
IMG_ROWS = 64
VIS_ALL = VIS_ROWS * CH
SIDE = 4
BLOCKS = SIDE * SIDE
ROWS = VIS_ROWS // IMG_ROWS
HALF = ROWS // 2
PACKED = 4 * HALF + 8
BEHIND = (0, -1, 1, 2)
FINE = 8
COARSE = GRID // 2 // FINE
XB = GRID // FINE
VALS = FACETS * TERMS
STEP = 2
LANES = 128
CHUNK = 104

COS = (0.99999999, -19.73920447, 64.93911593, -85.45011343, 60.16742979, -25.96688461, 6.52770596)
SIN = (6.28318491, -41.3415883, 81.59991362, -76.6141403, 41.34136538, -12.46881862)


def tables():
    gh = np.arange(COARSE)[:, None]
    xb = np.arange(XB)[None, :]
    ang = 2 * np.pi * ((gh * xb) % XB) / XB
    cosine, sine = np.cos(ang), np.sin(ang)
    first = np.concatenate(
        [np.concatenate([cosine, sine], 1), np.concatenate([-sine, cosine], 1)], 0
    )
    gl = np.arange(FINE)[:, None]
    tw = 2 * np.pi * (gl * xb) / GRID
    scale = np.where(gl % 2 == 0, 1.0, -1.0) / math.sqrt(VIS_ALL)
    twiddle = np.concatenate([np.cos(tw) * scale, np.sin(tw) * scale], 0)
    xa = np.arange(FINE)[:, None]
    turn = 2 * np.pi * ((xa * np.arange(FINE)[None, :]) % FINE) / FINE
    real, imag = np.cos(turn), -np.sin(turn)
    imag[:, 0] = 1.0
    eye = np.eye(VALS)
    second = np.concatenate([np.kron(eye, real), np.kron(eye, imag)], 1).astype(np.float32)
    second_high = second.astype(ml_dtypes.bfloat16)
    second_low = (second - second_high.astype(np.float32)).astype(ml_dtypes.bfloat16)
    return (
        jnp.asarray(first, jnp.bfloat16),
        jnp.asarray(twiddle, jnp.float32),
        (jnp.asarray(second_high), jnp.asarray(second_low)),
    )


def turns_cos_sin(turns):
    frac = turns - jnp.round(turns)
    sq = frac * frac
    cosine = jnp.full_like(sq, COS[-1])
    for coef in COS[-2::-1]:
        cosine = cosine * sq + coef
    sine = jnp.full_like(sq, SIN[-1])
    for coef in SIN[-2::-1]:
        sine = sine * sq + coef
    return cosine, sine * frac


def coded(cell):
    size = ((cell & 127) + 128) << ((cell >> 7) & 15)
    value = size.astype(jnp.float32)
    return jnp.where(cell >= GRID // 2, -value, value).astype(jnp.bfloat16)


def decoded(value):
    size = jnp.abs(value)
    high = jnp.where(value < 0.0, float(GRID // 2) - 128.0, -128.0)
    for step in (8, 4, 2, 1):
        over = size >= 128.0 * 2**step
        size = jnp.where(over, size * 2.0**-step, size)
        high = jnp.where(over, high + 128.0 * step, high)
    return size + high


def pack_kernel(
    vis_hbm, uv_hbm, cells_hbm, centre_hbm, out_ref, copy_ref, vis_ref, uv_ref, cells_ref, centre_ref, sems
):
    pairs = ((vis_hbm, vis_ref), (uv_hbm, uv_ref), (cells_hbm, cells_ref), (centre_hbm, centre_ref))
    copies = [pltpu.make_async_copy(a, b, sems.at[i]) for i, (a, b) in enumerate(pairs)]
    for i in (1, 3, 0, 2):
        copies[i].start()
    copies[1].wait()
    copies[3].wait()
    lane = lax.broadcasted_iota(jnp.int32, (HALF, 2 * CH), 1)

    def pieces(value):
        high = value.astype(jnp.bfloat16).astype(jnp.float32)
        rest = value - high
        mid = rest.astype(jnp.bfloat16).astype(jnp.float32)
        return high, mid, rest - mid

    split = jnp.concatenate(pieces(uv_ref[...]), 0).astype(jnp.bfloat16)
    spots = lax.broadcasted_iota(jnp.int32, (6, 2 * CH), 0)
    spots = spots == lax.broadcasted_iota(jnp.int32, (6, 2 * CH), 1)
    columns = lax.dot_general(
        split, spots.astype(jnp.float32).astype(jnp.bfloat16), (((0,), (0,)), ((), ())),
        preferred_element_type=jnp.float32,
    )
    whole = columns[0:8]
    for i in (1, 2, 3):
        whole = whole + pltpu.roll(columns[8 * i : 8 * i + 8], 32 * i, 1)
    cen = jnp.where(lane[0:8] % 2 == 0, centre_ref[0:1, 0:1], centre_ref[0:1, 1:2])
    for i, piece in enumerate(pieces(cen)):
        whole = jnp.where(lane[0:8] // 2 == 3 + i, piece, whole)
    out_ref[64:72] = whole.astype(jnp.bfloat16)
    copy_ref[...] = centre_ref[...]

    copies[0].wait()
    copies[2].wait()
    left = lane < CH
    vis = vis_ref[...].astype(jnp.float32)
    top, low = vis[:HALF], vis[HALF:]
    out_ref[0:16] = jnp.where(left, top, pltpu.roll(low, CH, 1)).astype(jnp.bfloat16)
    out_ref[16:32] = jnp.where(left, pltpu.roll(top, CH, 1), low).astype(jnp.bfloat16)
    for which in range(2):
        cells = cells_ref[which]
        both = jnp.concatenate([cells[:HALF], cells[HALF:]], 1)
        out_ref[32 + 16 * which : 48 + 16 * which] = coded(both)


def grid_kernel(
    blocks_ref, own_ref, pair_ref, first_hbm, twiddle_ref, high_ref, low_ref, o0, o1, o2, o3,
    terms0, terms1, cells0, cells1, total_ref, image_ref, iota_ref, first_ref, sem,
):
    table = pltpu.make_async_copy(first_hbm, first_ref, sem)
    table.start()
    own, row = lax.axis_index("facet"), lax.axis_index("vis")
    lane = lax.broadcasted_iota(jnp.int32, (HALF, 2 * CH), 1)
    chan = (lane % CH).astype(jnp.float32)
    nu = (2.0 * chan + 1.0 - CH) / CH
    freq = 1.0 + 0.15 * nu
    nu2 = nu * nu
    step = (row - IMG_ROWS // 2).astype(jnp.float32) * (1.0 / GRID)
    count = lax.broadcasted_iota(jnp.int32, (COARSE, 2 * CH), 0)
    iota_ref[...] = count.astype(jnp.float32).astype(jnp.bfloat16)
    fine_iota = count[:FINE].astype(jnp.float32)
    one = jnp.ones((2 * FINE, 2 * CH), jnp.bfloat16)
    zero = jnp.zeros((2 * FINE, 2 * CH), jnp.bfloat16)

    def joined(section):
        return section + pltpu.roll(section, 2 * CH - 2, 1) + pltpu.roll(section, 2 * CH - 4, 1)

    cens = []
    for y in range(2):
        sect = joined(blocks_ref[y * SIDE, 64:72].astype(jnp.float32))
        cens.append((sect[0:1, 6:7], sect[0:1, 7:8]))
    for ref in (own_ref, pair_ref):
        cens.append((ref[0:1, 0:1], ref[0:1, 1:2]))

    def elements(block, terms_ref, cell_ref):
        def section(at):
            return blocks_ref[block, 16 * at : 16 * at + 16].astype(jnp.float32)

        real, imag = section(0), section(1)
        gr, gc = decoded(section(2)), decoded(section(3))
        place = joined(blocks_ref[block, 64:72].astype(jnp.float32))
        is_left = lane[0:8] < CH

        def column(at):
            both = [
                jnp.where(is_left, place[:, i : i + 1], place[:, CH + i : CH + i + 1])
                for i in (at, at + 32)
            ]
            return jnp.concatenate(both, 0)

        u, v = column(0), column(1)
        mid = (gc == float(GRID // 2)).astype(jnp.float32)
        folded = jnp.where(gc > GRID // 2, GRID - gc, gc * (1.0 - mid))
        sign = jnp.where(gc > GRID // 2, -1.0, jnp.where(folded == 0.0, 0.0, 1.0))
        cell = folded.astype(jnp.int32)
        cell_ref[0] = (cell & (FINE - 1)).astype(jnp.float32)
        cell_ref[1] = (cell >> (FINE.bit_length() - 1)).astype(jnp.float32)
        keep = 1.0 - mid
        ca, sa = turns_cos_sin(gr * step)
        for q in range(SIDE):
            proj = u * cens[q][0] + v * cens[q][1]
            cp, sp = turns_cos_sin(proj * freq)
            rr = (real * cp + imag * sp).astype(jnp.bfloat16).astype(jnp.float32)
            ri = (imag * cp - real * sp).astype(jnp.bfloat16).astype(jnp.float32)
            br = ca * rr - sa * ri
            bi = ca * ri + sa * rr
            bi = bi * sign + br * mid
            br = br * keep
            terms_ref[q] = br
            terms_ref[SIDE + q] = bi

    def expand(i, terms_ref, cell_ref):
        fine = jnp.broadcast_to(cell_ref[0, i : i + 1, :], (FINE, 2 * CH)) == fine_iota
        left = []
        for k in range(FACETS):
            terms = []
            for base in (2 * k, 2 * k + 1):
                base = jnp.broadcast_to(terms_ref[base, i : i + 1, :], (FINE, 2 * CH))
                base = jnp.where(fine, base, 0.0)
                terms += [base, base * nu[:FINE], base * nu2[:FINE]]
            left.append(jnp.concatenate(terms, 0).astype(jnp.bfloat16))
        coarse = jnp.broadcast_to(cell_ref[1, i : i + 1, :], (2 * FINE, 2 * CH))
        coarse = coarse.astype(jnp.bfloat16)
        right = [
            jnp.where(coarse == iota_ref[m * 2 * FINE : (m + 1) * 2 * FINE], one, zero)
            for m in range(COARSE // (2 * FINE))
        ]
        return jnp.concatenate(left, 0), jnp.concatenate(right, 0)

    def turn(block, here, ahead):
        part = total_ref[...]
        elements(block, ahead[0], ahead[1])
        for i in range(0, HALF, STEP):
            both = [expand(i + j, here[0], here[1]) for j in range(STEP)]
            left = jnp.concatenate([sides[0] for sides in both], 1)
            right = jnp.concatenate([sides[1] for sides in both], 1)
            part = part + lax.dot_general(
                right, left, (((1,), (1,)), ((), ())), preferred_element_type=jnp.float32
            )
        total_ref[...] = part

    even, odd = (terms0, cells0), (terms1, cells1)
    total_ref[...] = jnp.zeros_like(total_ref)
    elements(0, terms0, cells0)

    def two(i, carry):
        turn(2 * i + 1, even, odd)
        turn(jnp.minimum(2 * i + 2, BLOCKS - 1), odd, even)
        return carry

    lax.fori_loop(0, BLOCKS // 2, two, 0, unroll=4)

    span = VALS * FINE
    flat = total_ref[...].T
    total = jnp.concatenate([flat[0:span], flat[span : 2 * span]], 1)
    table.wait()
    mixed = jnp.dot(total.astype(jnp.bfloat16), first_ref[...], preferred_element_type=jnp.float32)
    ur = mixed[:, :XB].reshape(VALS, FINE, XB)
    ui = mixed[:, XB:].reshape(VALS, FINE, XB)
    wr, wi = twiddle_ref[0:FINE][None], twiddle_ref[FINE : 2 * FINE][None]
    vr = ur * wr - ui * wi
    vi = ur * wi + ui * wr
    middle = total[:, COARSE : COARSE + 1].reshape(VALS, FINE, 1)
    is_odd = lax.broadcasted_iota(jnp.int32, (1, 1, XB), 2) % 2 == 1
    flip = jnp.where(is_odd, -1.0, 1.0) * (1.0 / math.sqrt(VIS_ALL))
    at_zero = lax.broadcasted_iota(jnp.int32, (1, FINE, XB), 1) == 0
    vi = jnp.where(at_zero, middle * flip, vi)
    both = jnp.concatenate([vr.reshape(span, XB), vi.reshape(span, XB)], 0)
    high = both.astype(jnp.bfloat16)
    low = (both - high.astype(jnp.float32)).astype(jnp.bfloat16)
    image = jnp.dot(high_ref[...], high, preferred_element_type=jnp.float32)
    image = image + jnp.dot(high_ref[...], low, preferred_element_type=jnp.float32)
    image = image + jnp.dot(low_ref[...], high, preferred_element_type=jnp.float32)
    image_ref[...] = image
    size = TERMS * FINE
    for s, out in enumerate((o0, o1, o2, o3)):
        spot = (2, 3, 1, 0)[s]
        before = ((own ^ s) + FACETS - 1) % FACETS ^ own
        before = jnp.where(before < 2, before + 2, 3 - before)
        mine = image_ref[spot * size : (spot + 1) * size]
        prior = image_ref[pl.ds(pl.multiple_of(before * size, 8), size), :]
        for c in range(XB // LANES):
            out[c * size : (c + 1) * size] = mine[:, c * LANES : (c + 1) * LANES].astype(out.dtype)
        strips = [
            prior[term * FINE + FINE - 1 : term * FINE + FINE, at : at + LANES]
            for at in range(XB - OVER, XB, LANES)
            for term in range(TERMS)
        ]
        strips = jnp.concatenate(strips + [jnp.zeros((2, LANES), jnp.float32)], 0)
        out[CHUNK - 8 : CHUNK] = strips.astype(out.dtype)


def blend_kernel(p0, p1, p2, p3, mask_ref, out_hbm, out_ref, sems):
    size = TERMS * FINE
    image = p0[...]
    for part in (p1, p2, p3):
        image = image + part[...].astype(jnp.float32)
    has_left = (lax.axis_index("facet") > 0).astype(jnp.float32)
    pixel = lax.broadcasted_iota(jnp.int32, (1, OVER), 1).astype(jnp.float32)
    ramp = 1.0 - (pixel + 0.5) / OVER
    weight = mask_ref[0].astype(jnp.float32) * ramp * has_left
    copies = []
    for term in range(TERMS):
        for xa in range(FINE):
            for c in range(XB // LANES):
                row = c * size + term * FINE + xa
                line = image[row : row + 1]
                if xa == 0 and c < OVER // LANES:
                    at = CHUNK - 8 + c * TERMS + term
                    strip = image[at : at + 1]
                    line = line + weight[:, c * LANES : (c + 1) * LANES] * (strip - line)
                at = xa * XB + c * LANES
                out_ref[term, :, at : at + LANES] = line
        copies.append(pltpu.make_async_copy(out_ref.at[term], out_hbm.at[term], sems.at[term]))
        copies[-1].start()
    for copy in copies:
        copy.wait()


def swap_pairs():
    pairs = []
    for facet in range(FACETS):
        for z in range(SIDE):
            for y in range(SIDE):
                for x in range(SIDE):
                    here = y * SIDE + x
                    plane = (z + BEHIND[facet]) % SIDE
                    source = ((3 - facet) ^ (y & 1)) * IMG_ROWS + plane * BLOCKS + here
                    pairs.append((source, facet * IMG_ROWS + z * BLOCKS + here))
    return pairs


def partial_images(blocks, centres, pair):
    vmem = pl.BlockSpec(memory_space=pltpu.VMEM)
    hbm = pl.BlockSpec(memory_space=pltpu.HBM)
    first, twiddle, second = tables()
    first = pltpu.with_memory_space_constraint(first, pltpu.HBM)
    chunk = [
        jax.ShapeDtypeStruct((CHUNK, LANES), jnp.bfloat16 if s else jnp.float32)
        for s in range(FACETS)
    ]
    span = 2 * VALS * FINE
    return pl.pallas_call(
        grid_kernel,
        out_shape=chunk,
        in_specs=[vmem] * 3 + [hbm] + [vmem] * 3,
        out_specs=[vmem] * FACETS,
        scratch_shapes=[
            pltpu.VMEM((2 * FACETS, HALF, 2 * CH), jnp.float32),
            pltpu.VMEM((2 * FACETS, HALF, 2 * CH), jnp.float32),
            pltpu.VMEM((2, HALF, 2 * CH), jnp.float32),
            pltpu.VMEM((2, HALF, 2 * CH), jnp.float32),
            pltpu.VMEM((COARSE, span), jnp.float32),
            pltpu.VMEM((VALS * FINE, XB), jnp.float32),
            pltpu.VMEM((COARSE, 2 * CH), jnp.bfloat16),
            pltpu.VMEM((2 * COARSE, 2 * XB), jnp.bfloat16),
            pltpu.SemaphoreType.DMA,
        ],
        compiler_params=pltpu.CompilerParams(vmem_limit_bytes=16 << 20),
        name="grid",
    )(blocks, centres, pair, first, twiddle, *second)


def per_device(visibilities, uv_coords, cells, centres, intersection_mask):
    vmem = pl.BlockSpec(memory_space=pltpu.VMEM)
    hbm = pl.BlockSpec(memory_space=pltpu.HBM)
    given = (visibilities, uv_coords.T, cells, centres)
    given = [pltpu.with_memory_space_constraint(one, pltpu.HBM) for one in given]
    packed, centre = pl.pallas_call(
        pack_kernel,
        out_shape=[
            jax.ShapeDtypeStruct((PACKED, 2 * CH), jnp.bfloat16),
            jax.ShapeDtypeStruct((1, 2), jnp.float32),
        ],
        in_specs=[hbm] * 4,
        out_specs=[vmem] * 2,
        scratch_shapes=[pltpu.VMEM(one.shape, one.dtype) for one in given]
        + [pltpu.SemaphoreType.DMA((4,))],
        compiler_params=pltpu.CompilerParams(vmem_limit_bytes=2 << 20),
        name="pack",
    )(*given)
    pair = lax.ppermute(centre, "facet", [(i, i ^ 1) for i in range(FACETS)])
    packed = lax.ppermute(packed, ("facet", "vis"), swap_pairs())
    packed, pair = lax.optimization_barrier((packed, pair))
    planes = [[z * BLOCKS + i for i in range(BLOCKS)] for z in range(SIDE)]
    blocks = lax.all_to_all(
        jnp.broadcast_to(packed[None], (BLOCKS,) + packed.shape),
        "vis", 0, 0, axis_index_groups=planes,
    )
    parts = partial_images(blocks, centre, pair)
    got = [parts[0]]
    for s in (3, 2, 1):
        got.append(lax.ppermute(parts[s], "facet", [(i, i ^ s) for i in range(FACETS)]))
    return pl.pallas_call(
        blend_kernel,
        out_shape=jax.ShapeDtypeStruct((TERMS, 1, GRID), jnp.float32),
        in_specs=[vmem] * 5,
        out_specs=hbm,
        scratch_shapes=[
            pltpu.VMEM((TERMS, 1, GRID), jnp.float32),
            pltpu.SemaphoreType.DMA((TERMS,)),
        ],
        compiler_params=pltpu.CompilerParams(vmem_limit_bytes=2 << 20),
        name="blend",
    )(*got, intersection_mask)


def solution(mesh):
    placed = (
        P("vis", None),
        P("vis", None),
        P(None, "vis", None),
        P("facet", None),
        P("facet", "vis", None),
    )
    return jax.shard_map(
        per_device, mesh=mesh, in_specs=placed, out_specs=P(None, "vis", "facet"), check_vma=False
    )
```

```python
import math

import jax
import jax.numpy as jnp
import ml_dtypes
import numpy as np
from jax import lax
from jax.experimental import pallas as pl
from jax.experimental.pallas import tpu as pltpu
from jax.sharding import PartitionSpec as P

GRID = 4096
CH = 64
TERMS = 3
OVER = 256
FACETS = 4
VIS_ROWS = 2048
IMG_ROWS = 64
VIS_ALL = VIS_ROWS * CH
SIDE = 4
BLOCKS = SIDE * SIDE
ROWS = VIS_ROWS // IMG_ROWS
HALF = ROWS // 2
PACKED = 4 * HALF + 8
BEHIND = (0, -1, 1, 2)
FINE = 8
COARSE = GRID // 2 // FINE
XB = GRID // FINE
VALS = FACETS * TERMS
STEP = 2
LANES = 128
CHUNK = 104

COS = (0.99999999, -19.73920447, 64.93911593, -85.45011343, 60.16742979, -25.96688461, 6.52770596)
SIN = (6.28318491, -41.3415883, 81.59991362, -76.6141403, 41.34136538, -12.46881862)


def tables():
    gh = np.arange(COARSE)[:, None]
    xb = np.arange(XB)[None, :]
    ang = 2 * np.pi * ((gh * xb) % XB) / XB
    cosine, sine = np.cos(ang), np.sin(ang)
    first = np.concatenate(
        [np.concatenate([cosine, sine], 1), np.concatenate([-sine, cosine], 1)], 0
    )
    gl = np.arange(FINE)[:, None]
    tw = 2 * np.pi * (gl * xb) / GRID
    scale = np.where(gl % 2 == 0, 1.0, -1.0) / math.sqrt(VIS_ALL)
    twiddle = np.concatenate([np.cos(tw) * scale, np.sin(tw) * scale], 0)
    xa = np.arange(FINE)[:, None]
    turn = 2 * np.pi * ((xa * np.arange(FINE)[None, :]) % FINE) / FINE
    real, imag = np.cos(turn), -np.sin(turn)
    imag[:, 0] = 1.0
    eye = np.eye(VALS)
    second = np.concatenate([np.kron(eye, real), np.kron(eye, imag)], 1).astype(np.float32)
    second_high = second.astype(ml_dtypes.bfloat16)
    second_low = (second - second_high.astype(np.float32)).astype(ml_dtypes.bfloat16)
    return (
        jnp.asarray(first, jnp.bfloat16),
        jnp.asarray(twiddle, jnp.float32),
        (jnp.asarray(second_high), jnp.asarray(second_low)),
    )


def turns_cos_sin(turns):
    frac = turns - jnp.round(turns)
    sq = frac * frac
    cosine = jnp.full_like(sq, COS[-1])
    for coef in COS[-2::-1]:
        cosine = cosine * sq + coef
    sine = jnp.full_like(sq, SIN[-1])
    for coef in SIN[-2::-1]:
        sine = sine * sq + coef
    return cosine, sine * frac


def coded(cell):
    size = ((cell & 127) + 128) << ((cell >> 7) & 15)
    value = size.astype(jnp.float32)
    return jnp.where(cell >= GRID // 2, -value, value).astype(jnp.bfloat16)


def decoded(value):
    size = jnp.abs(value)
    high = jnp.where(value < 0.0, float(GRID // 2) - 128.0, -128.0)
    for step in (8, 4, 2, 1):
        over = size >= 128.0 * 2**step
        size = jnp.where(over, size * 2.0**-step, size)
        high = jnp.where(over, high + 128.0 * step, high)
    return size + high


def pack_kernel(
    vis_hbm, uv_hbm, cells_hbm, centre_hbm, out_ref, copy_ref, vis_ref, uv_ref, cells_ref, centre_ref, sems
):
    pairs = ((vis_hbm, vis_ref), (uv_hbm, uv_ref), (cells_hbm, cells_ref), (centre_hbm, centre_ref))
    copies = [pltpu.make_async_copy(a, b, sems.at[i]) for i, (a, b) in enumerate(pairs)]
    for i in (1, 3, 0, 2):
        copies[i].start()
    copies[1].wait()
    copies[3].wait()
    lane = lax.broadcasted_iota(jnp.int32, (HALF, 2 * CH), 1)

    def pieces(value):
        high = value.astype(jnp.bfloat16).astype(jnp.float32)
        rest = value - high
        mid = rest.astype(jnp.bfloat16).astype(jnp.float32)
        return high, mid, rest - mid

    split = jnp.concatenate(pieces(uv_ref[...]), 0).astype(jnp.bfloat16)
    spots = lax.broadcasted_iota(jnp.int32, (6, 2 * CH), 0)
    spots = spots == lax.broadcasted_iota(jnp.int32, (6, 2 * CH), 1)
    columns = lax.dot_general(
        split, spots.astype(jnp.float32).astype(jnp.bfloat16), (((0,), (0,)), ((), ())),
        preferred_element_type=jnp.float32,
    )
    whole = columns[0:8]
    for i in (1, 2, 3):
        whole = whole + pltpu.roll(columns[8 * i : 8 * i + 8], 32 * i, 1)
    cen = jnp.where(lane[0:8] % 2 == 0, centre_ref[0:1, 0:1], centre_ref[0:1, 1:2])
    for i, piece in enumerate(pieces(cen)):
        whole = jnp.where(lane[0:8] // 2 == 3 + i, piece, whole)
    out_ref[64:72] = whole.astype(jnp.bfloat16)
    copy_ref[...] = centre_ref[...]

    copies[0].wait()
    copies[2].wait()
    left = lane < CH
    vis = vis_ref[...].astype(jnp.float32)
    top, low = vis[:HALF], vis[HALF:]
    out_ref[0:16] = jnp.where(left, top, pltpu.roll(low, CH, 1)).astype(jnp.bfloat16)
    out_ref[16:32] = jnp.where(left, pltpu.roll(top, CH, 1), low).astype(jnp.bfloat16)
    for which in range(2):
        cells = cells_ref[which]
        both = jnp.concatenate([cells[:HALF], cells[HALF:]], 1)
        out_ref[32 + 16 * which : 48 + 16 * which] = coded(both)


def grid_kernel(
    blocks_ref, own_ref, pair_ref, first_hbm, twiddle_ref, high_ref, low_ref, o0, o1, o2, o3,
    terms0, terms1, cells0, cells1, total_ref, image_ref, iota_ref, first_ref, sem,
):
    table = pltpu.make_async_copy(first_hbm, first_ref, sem)
    table.start()
    own, row = lax.axis_index("facet"), lax.axis_index("vis")
    lane = lax.broadcasted_iota(jnp.int32, (HALF, 2 * CH), 1)
    chan = (lane % CH).astype(jnp.float32)
    nu = (2.0 * chan + 1.0 - CH) / CH
    freq = 1.0 + 0.15 * nu
    nu2 = nu * nu
    step = (row - IMG_ROWS // 2).astype(jnp.float32) * (1.0 / GRID)
    count = lax.broadcasted_iota(jnp.int32, (COARSE, 2 * CH), 0)
    iota_ref[...] = count.astype(jnp.float32).astype(jnp.bfloat16)
    fine_iota = count[:FINE].astype(jnp.float32)
    one = jnp.ones((2 * FINE, 2 * CH), jnp.bfloat16)
    zero = jnp.zeros((2 * FINE, 2 * CH), jnp.bfloat16)

    def joined(section):
        return section + pltpu.roll(section, 2 * CH - 2, 1) + pltpu.roll(section, 2 * CH - 4, 1)

    cens = []
    for y in range(2):
        sect = joined(blocks_ref[y * SIDE, 64:72].astype(jnp.float32))
        cens.append((sect[0:1, 6:7], sect[0:1, 7:8]))
    for ref in (own_ref, pair_ref):
        cens.append((ref[0:1, 0:1], ref[0:1, 1:2]))

    def elements(block, terms_ref, cell_ref):
        def section(at):
            return blocks_ref[block, 16 * at : 16 * at + 16].astype(jnp.float32)

        real, imag = section(0), section(1)
        gr, gc = decoded(section(2)), decoded(section(3))
        place = joined(blocks_ref[block, 64:72].astype(jnp.float32))
        is_left = lane[0:8] < CH

        def column(at):
            both = [
                jnp.where(is_left, place[:, i : i + 1], place[:, CH + i : CH + i + 1])
                for i in (at, at + 32)
            ]
            return jnp.concatenate(both, 0)

        u, v = column(0), column(1)
        mid = (gc == float(GRID // 2)).astype(jnp.float32)
        folded = jnp.where(gc > GRID // 2, GRID - gc, gc * (1.0 - mid))
        sign = jnp.where(gc > GRID // 2, -1.0, jnp.where(folded == 0.0, 0.0, 1.0))
        cell = folded.astype(jnp.int32)
        cell_ref[0] = (cell & (FINE - 1)).astype(jnp.float32)
        cell_ref[1] = (cell >> (FINE.bit_length() - 1)).astype(jnp.float32)
        keep = 1.0 - mid
        ca, sa = turns_cos_sin(gr * step)
        for q in range(SIDE):
            proj = u * cens[q][0] + v * cens[q][1]
            cp, sp = turns_cos_sin(proj * freq)
            rr = (real * cp + imag * sp).astype(jnp.bfloat16).astype(jnp.float32)
            ri = (imag * cp - real * sp).astype(jnp.bfloat16).astype(jnp.float32)
            br = ca * rr - sa * ri
            bi = ca * ri + sa * rr
            bi = bi * sign + br * mid
            br = br * keep
            terms_ref[q] = br
            terms_ref[SIDE + q] = bi

    def expand(i, terms_ref, cell_ref):
        fine = jnp.broadcast_to(cell_ref[0, i : i + 1, :], (FINE, 2 * CH)) == fine_iota
        left = []
        for k in range(FACETS):
            terms = []
            for base in (2 * k, 2 * k + 1):
                base = jnp.broadcast_to(terms_ref[base, i : i + 1, :], (FINE, 2 * CH))
                base = jnp.where(fine, base, 0.0)
                terms += [base, base * nu[:FINE], base * nu2[:FINE]]
            left.append(jnp.concatenate(terms, 0).astype(jnp.bfloat16))
        coarse = jnp.broadcast_to(cell_ref[1, i : i + 1, :], (2 * FINE, 2 * CH))
        coarse = coarse.astype(jnp.bfloat16)
        right = [
            jnp.where(coarse == iota_ref[m * 2 * FINE : (m + 1) * 2 * FINE], one, zero)
            for m in range(COARSE // (2 * FINE))
        ]
        return jnp.concatenate(left, 0), jnp.concatenate(right, 0)

    def turn(block, here, ahead):
        part = total_ref[...]
        elements(block, ahead[0], ahead[1])
        for i in range(0, HALF, STEP):
            both = [expand(i + j, here[0], here[1]) for j in range(STEP)]
            left = jnp.concatenate([sides[0] for sides in both], 1)
            right = jnp.concatenate([sides[1] for sides in both], 1)
            part = part + lax.dot_general(
                right, left, (((1,), (1,)), ((), ())), preferred_element_type=jnp.float32
            )
        total_ref[...] = part

    even, odd = (terms0, cells0), (terms1, cells1)
    total_ref[...] = jnp.zeros_like(total_ref)
    elements(0, terms0, cells0)

    def two(i, carry):
        turn(2 * i + 1, even, odd)
        turn(jnp.minimum(2 * i + 2, BLOCKS - 1), odd, even)
        return carry

    lax.fori_loop(0, BLOCKS // 2, two, 0, unroll=4)

    span = VALS * FINE
    flat = total_ref[...].T
    total = jnp.concatenate([flat[0:span], flat[span : 2 * span]], 1)
    table.wait()
    mixed = jnp.dot(total.astype(jnp.bfloat16), first_ref[...], preferred_element_type=jnp.float32)
    ur = mixed[:, :XB].reshape(VALS, FINE, XB)
    ui = mixed[:, XB:].reshape(VALS, FINE, XB)
    wr, wi = twiddle_ref[0:FINE][None], twiddle_ref[FINE : 2 * FINE][None]
    vr = ur * wr - ui * wi
    vi = ur * wi + ui * wr
    middle = total[:, COARSE : COARSE + 1].reshape(VALS, FINE, 1)
    is_odd = lax.broadcasted_iota(jnp.int32, (1, 1, XB), 2) % 2 == 1
    flip = jnp.where(is_odd, -1.0, 1.0) * (1.0 / math.sqrt(VIS_ALL))
    at_zero = lax.broadcasted_iota(jnp.int32, (1, FINE, XB), 1) == 0
    vi = jnp.where(at_zero, middle * flip, vi)
    both = jnp.concatenate([vr.reshape(span, XB), vi.reshape(span, XB)], 0)
    high = both.astype(jnp.bfloat16)
    low = (both - high.astype(jnp.float32)).astype(jnp.bfloat16)
    stages = jnp.concatenate([high_ref[...], low_ref[...]], 0)
    image = jnp.dot(stages, high, preferred_element_type=jnp.float32)
    image = image[:span] + image[span:]
    image = image + jnp.dot(high_ref[...], low, preferred_element_type=jnp.float32)
    image_ref[...] = image
    size = TERMS * FINE
    for s, out in enumerate((o0, o1, o2, o3)):
        spot = (2, 3, 1, 0)[s]
        before = ((own ^ s) + FACETS - 1) % FACETS ^ own
        before = jnp.where(before < 2, before + 2, 3 - before)
        mine = image_ref[spot * size : (spot + 1) * size]
        prior = image_ref[pl.ds(pl.multiple_of(before * size, 8), size), :]
        for c in range(XB // LANES):
            out[c * size : (c + 1) * size] = mine[:, c * LANES : (c + 1) * LANES].astype(out.dtype)
        strips = [
            prior[term * FINE + FINE - 1 : term * FINE + FINE, at : at + LANES]
            for at in range(XB - OVER, XB, LANES)
            for term in range(TERMS)
        ]
        strips = jnp.concatenate(strips + [jnp.zeros((2, LANES), jnp.float32)], 0)
        out[CHUNK - 8 : CHUNK] = strips.astype(out.dtype)


def blend_kernel(p0, p1, p2, p3, mask_ref, out_ref):
    size = TERMS * FINE
    image = p0[...]
    for part in (p1, p2, p3):
        image = image + part[...].astype(jnp.float32)
    has_left = (lax.axis_index("facet") > 0).astype(jnp.float32)
    pixel = lax.broadcasted_iota(jnp.int32, (1, OVER), 1).astype(jnp.float32)
    ramp = 1.0 - (pixel + 0.5) / OVER
    weight = mask_ref[0].astype(jnp.float32) * ramp * has_left
    for term in range(TERMS):
        for xa in range(FINE):
            for c in range(XB // LANES):
                row = c * size + term * FINE + xa
                line = image[row : row + 1]
                if xa == 0 and c < OVER // LANES:
                    at = CHUNK - 8 + c * TERMS + term
                    strip = image[at : at + 1]
                    line = line + weight[:, c * LANES : (c + 1) * LANES] * (strip - line)
                at = xa * XB + c * LANES
                out_ref[term, :, at : at + LANES] = line


def swap_pairs():
    pairs = []
    for facet in range(FACETS):
        for z in range(SIDE):
            for y in range(SIDE):
                for x in range(SIDE):
                    here = y * SIDE + x
                    plane = (z + BEHIND[facet]) % SIDE
                    source = ((3 - facet) ^ (y & 1)) * IMG_ROWS + plane * BLOCKS + here
                    pairs.append((source, facet * IMG_ROWS + z * BLOCKS + here))
    return pairs


def partial_images(blocks, centres, pair):
    vmem = pl.BlockSpec(memory_space=pltpu.VMEM)
    hbm = pl.BlockSpec(memory_space=pltpu.HBM)
    first, twiddle, second = tables()
    first = pltpu.with_memory_space_constraint(first, pltpu.HBM)
    chunk = [
        jax.ShapeDtypeStruct((CHUNK, LANES), jnp.bfloat16 if s else jnp.float32)
        for s in range(FACETS)
    ]
    span = 2 * VALS * FINE
    return pl.pallas_call(
        grid_kernel,
        out_shape=chunk,
        in_specs=[vmem] * 3 + [hbm] + [vmem] * 3,
        out_specs=[vmem] * FACETS,
        scratch_shapes=[
            pltpu.VMEM((2 * FACETS, HALF, 2 * CH), jnp.float32),
            pltpu.VMEM((2 * FACETS, HALF, 2 * CH), jnp.float32),
            pltpu.VMEM((2, HALF, 2 * CH), jnp.float32),
            pltpu.VMEM((2, HALF, 2 * CH), jnp.float32),
            pltpu.VMEM((COARSE, span), jnp.float32),
            pltpu.VMEM((VALS * FINE, XB), jnp.float32),
            pltpu.VMEM((COARSE, 2 * CH), jnp.bfloat16),
            pltpu.VMEM((2 * COARSE, 2 * XB), jnp.bfloat16),
            pltpu.SemaphoreType.DMA,
        ],
        compiler_params=pltpu.CompilerParams(vmem_limit_bytes=16 << 20),
        name="grid",
    )(blocks, centres, pair, first, twiddle, *second)


def per_device(visibilities, uv_coords, cells, centres, intersection_mask):
    vmem = pl.BlockSpec(memory_space=pltpu.VMEM)
    hbm = pl.BlockSpec(memory_space=pltpu.HBM)
    given = (visibilities, uv_coords.T, cells, centres)
    given = [pltpu.with_memory_space_constraint(one, pltpu.HBM) for one in given]
    packed, centre = pl.pallas_call(
        pack_kernel,
        out_shape=[
            jax.ShapeDtypeStruct((PACKED, 2 * CH), jnp.bfloat16),
            jax.ShapeDtypeStruct((1, 2), jnp.float32),
        ],
        in_specs=[hbm] * 4,
        out_specs=[vmem] * 2,
        scratch_shapes=[pltpu.VMEM(one.shape, one.dtype) for one in given]
        + [pltpu.SemaphoreType.DMA((4,))],
        compiler_params=pltpu.CompilerParams(vmem_limit_bytes=2 << 20),
        name="pack",
    )(*given)
    pair = lax.ppermute(centre, "facet", [(i, i ^ 1) for i in range(FACETS)])
    packed = lax.ppermute(packed, ("facet", "vis"), swap_pairs())
    packed, pair = lax.optimization_barrier((packed, pair))
    planes = [[z * BLOCKS + i for i in range(BLOCKS)] for z in range(SIDE)]
    blocks = lax.all_to_all(
        jnp.broadcast_to(packed[None], (BLOCKS,) + packed.shape),
        "vis", 0, 0, axis_index_groups=planes,
    )
    parts = partial_images(blocks, centre, pair)
    got = [parts[0]]
    for s in (3, 2, 1):
        got.append(lax.ppermute(parts[s], "facet", [(i, i ^ s) for i in range(FACETS)]))
    return pl.pallas_call(
        blend_kernel,
        out_shape=jax.ShapeDtypeStruct((TERMS, 1, GRID), jnp.float32),
        in_specs=[vmem] * 5,
        out_specs=vmem,
        compiler_params=pltpu.CompilerParams(vmem_limit_bytes=2 << 20),
        name="blend",
    )(*got, intersection_mask)


def solution(mesh):
    placed = (
        P("vis", None),
        P("vis", None),
        P(None, "vis", None),
        P("facet", None),
        P("facet", "vis", None),
    )
    return jax.shard_map(
        per_device, mesh=mesh, in_specs=placed, out_specs=P(None, "vis", "facet"), check_vma=False
    )
```
